128 devices in a mesh: tm: 4 (over x), space: 32 (over y, z, core).
Axes of the slice: x: 4, y: 4, z: 4, core: 2. Of those that a mesh axis runs over, the one named last changes fastest.
Arguments:
- pixel_cot: bfloat16 [16, 256, 64, 128], P('tm', 'space'), may hold values from -6 to 6
- frame_group: int32 [16], P('tm'), may hold values from 0 to 3
- advantage: float32 [4], replicated, may hold values from -4 to 4
- block_in: bfloat16 [2, 16, 256, 64, 128], P(None, 'tm', 'space'), may hold values from -6 to 6
- conv1_weight: bfloat16 [2, 3, 3, 3, 128, 128], replicated, may hold values from -0.109375 to 0.109375
- conv2_weight: bfloat16 [2, 3, 3, 3, 128, 128], replicated, may hold values from -0.109375 to 0.109375
- owner_map: int32 [4, 32, 64, 1], P('tm', 'space'), may hold values from 0 to 31; in each aligned block of 64 rows (0 to 63, 64 to 127, ..., all dimensions but the last counted through in order) at most 4 rows name the same one
Outputs:
- latent_grad: bfloat16 [4, 32, 32, 4, 1024], P('tm', 'space')
The draws below stay inside these ranges and needn't reach their ends.
Inputs may be any that keep to these rules, and one draw needn't show every extreme that they name: `owner_map`: among the units of one device, at most 4 have the same owner, and in some devices exactly 4 do.
All inputs are finite; a program needn't handle non-finite values.
Results may differ from the reference program's by a relative error of at most 0.013.
Values may be sent and summed in bfloat16 or wider, within the bound.
No kernel may reach another device: no remote copies, remote signals or barrier semaphores. Data moves between devices by JAX's collectives and lax.ppermute only.
A program may use at most 128 MiB of HBM per device.

```python
import math
import jax
import jax.numpy as jnp
import numpy as np
from jax import lax

CHAN = 128
BLOCKS = 2
GROUPS = 4
FRAME_DEV = 4
STRIP = 8
COLS = 64
FRAMES = 16
ROWS = 256
UNITS = 64
CAP = 4
N_TM = 4
N_SPACE = 32


def set_ends(drawn, rng, smallest, top_value):
    index_at = [jax.random.randint(jax.random.fold_in(rng, axis), (), 0, length) for axis, length in enumerate(drawn.shape)]
    longest = drawn.shape.index(max(drawn.shape))
    neighbour = index_at[:longest] + [(index_at[longest] + 1) % drawn.shape[longest]] + index_at[longest + 1:]
    return drawn.at[tuple(index_at)].set(smallest).at[tuple(neighbour)].set(top_value)


def block_scale(key, extent, shards, low, largest):
    level, own = 1.0, jax.random.fold_in(key, 6)
    for axis_at, parts in shards:
        steps = jnp.exp(jax.random.uniform(jax.random.fold_in(own, axis_at), (parts,), jnp.float32, low / len(shards), largest / len(shards)))
        level = level * jnp.repeat(steps, extent[axis_at] // parts).reshape([-1 if axis == axis_at else 1 for axis in range(len(extent))])
    return level


def routed_block(rng, own, number, rows, count, top, reach, lean):
    sequence = jax.random.permutation(rng, count)
    heavy_load, ordinary = portions_of(count, rows * top, reach, lean, True), portions_of(count, rows * top, reach, lean, False)
    places = jnp.arange(count)

    def named(lengths, offset_by):
        used = int((lengths > 0).sum())
        fixed = max(1, used // 4)
        passed = fixed + (places - fixed + offset_by * (used - fixed)) % max(1, count - fixed)
        return jnp.zeros((count,), jnp.int32).at[sequence[jnp.where(places < fixed, places, passed)]].set(jnp.asarray(lengths, jnp.int32))

    lengths = jnp.where(number % 4 == 0, named(heavy_load, number // 4), named(ordinary, number - number // 4 - 1))
    mixed = jax.random.permutation(jax.random.fold_in(own, 3), count)
    donor, receiver = mixed[0:count // 2 * 2:2], mixed[1:count // 2 * 2:2]
    slack = jnp.minimum(lengths[donor] - 1, reach - lengths[receiver]) // 2
    slack = jnp.where((donor == sequence[0]) | (receiver == sequence[0]) | (lengths[receiver] == 0), 0, jnp.maximum(slack, 0))
    passed = jax.random.randint(jax.random.fold_in(own, 4), (count // 2,), 0, 1 << 20) % (slack + 1)
    lengths = lengths.at[donor].add(-passed).at[receiver].add(passed)
    members = jnp.searchsorted(jnp.cumsum(lengths), jnp.arange(rows * top), side="right").astype(jnp.int32)
    grid = members.reshape(top, rows).T
    grid = grid[jax.random.permutation(jax.random.fold_in(own, 1), rows)]
    offset_by = jax.random.randint(jax.random.fold_in(own, 2), (rows, 1), 0, top)
    return jnp.take_along_axis(grid, (jnp.arange(top)[None, :] + offset_by) % top, axis=1)


def portions_of(amount, total, reach, slope, full):
    portions = [(1 << 20) // math.isqrt(standing ** slope) + 1 for standing in range(1, amount + 1)]
    largest = reach if full else min(reach, max(-(-total // amount), total * portions[0] // sum(portions)))
    least = 1 if total - largest >= amount - 1 else 0
    counts, rest = [largest] + [least] * (amount - 1), total - largest - least * (amount - 1)
    while rest > 0:
        candidates = [i for i in range(1, amount) if counts[i] < largest] or [i for i in range(1, amount) if counts[i] < reach]
        pool, remaining = sum([portions[i] for i in candidates]), rest
        for i in candidates:
            more = min(reach - counts[i], max(1, remaining * portions[i] // pool), rest)
            counts[i] = counts[i] + more
            rest = rest - more
    return np.array(counts)


def gaussian(stream_key, shape, scale, reach, cuts=(), kind=jnp.bfloat16):
    array = jax.random.normal(stream_key, shape, jnp.float32) * scale
    if len(cuts) > 0:
        array = block_scale(stream_key, shape, cuts, -0.22, 0.18) * array
    return jnp.clip(array, min=-reach, max=reach).astype(kind)


def setup_inputs(seed: int = 0) -> dict:
    key_list = jax.random.split(jax.random.key(seed), 8)
    pixel_cot = gaussian(key_list[0], (FRAMES, ROWS, COLS, CHAN), 1.0, 6.0, ((0, 4), (1, 32)))
    frame_group = set_ends(jax.random.randint(key_list[1], (FRAMES,), 0, GROUPS), jax.random.fold_in(key_list[1], 1), 0, GROUPS - 1).astype(jnp.int32)
    advantage = gaussian(key_list[2], (GROUPS,), 1.0, 4.0, (), jnp.float32)
    block_in = gaussian(key_list[3], (BLOCKS, FRAMES, ROWS, COLS, CHAN), 1.0, 6.0, ((1, 4), (2, 32)))
    conv1_weight = gaussian(key_list[4], (BLOCKS, 3, 3, 3, CHAN, CHAN), (27 * CHAN) ** -0.5, 0.109375)
    conv2_weight = gaussian(key_list[5], (BLOCKS, 3, 3, 3, CHAN, CHAN), (27 * CHAN) ** -0.5, 0.109375)
    owner_map_keys = jax.random.split(jax.random.fold_in(key_list[6], 1), N_TM * N_SPACE * UNITS // UNITS)
    owner_map_turns = jax.random.permutation(jax.random.fold_in(key_list[6], 3), N_TM * N_SPACE * UNITS // UNITS)
    owner_map = jax.vmap(lambda own, number: routed_block(jax.random.fold_in(key_list[6], 2), own, number, UNITS, N_SPACE, 1, CAP, 1))(owner_map_keys, owner_map_turns).reshape((N_TM, N_SPACE, UNITS, 1))
    return {"pixel_cot": pixel_cot, "frame_group": frame_group, "advantage": advantage, "block_in": block_in, "conv1_weight": conv1_weight, "conv2_weight": conv2_weight, "owner_map": owner_map}


def conv_forward(field, kernel):
    return lax.conv_general_dilated(field[None], kernel, (1, 1, 1), ((2, 0), (1, 1), (1, 1)), dimension_numbers=("NDHWC", "DHWIO", "NDHWC"), precision=lax.Precision.HIGHEST)[0]


def conv_backward(field, kernel):
    flipped = jnp.swapaxes(jnp.flip(kernel, (0, 1, 2)), 3, 4)
    return lax.conv_general_dilated(field[None], flipped, (1, 1, 1), ((0, 2), (1, 1), (1, 1)), dimension_numbers=("NDHWC", "DHWIO", "NDHWC"), precision=lax.Precision.HIGHEST)[0]


def reference(pixel_cot, frame_group, advantage, block_in, conv1_weight, conv2_weight, owner_map):
    frame_scale = advantage[frame_group]
    upstream = (pixel_cot.astype(jnp.float32) * frame_scale[:, None, None, None]).astype(jnp.bfloat16)
    for layer in reversed(range(BLOCKS)):
        inputs = block_in[layer].astype(jnp.float32)
        hidden_pre = conv_forward(inputs, conv1_weight[layer].astype(jnp.float32))
        grad_act = conv_backward(upstream.astype(jnp.float32), conv2_weight[layer].astype(jnp.float32))
        sigma = jax.nn.sigmoid(hidden_pre)
        grad_pre = (grad_act * (sigma * (1.0 + hidden_pre * (1.0 - sigma)))).astype(jnp.bfloat16)
        back = conv_backward(grad_pre.astype(jnp.float32), conv1_weight[layer].astype(jnp.float32))
        upstream = (upstream.astype(jnp.float32) + back).astype(jnp.bfloat16)
    pooled = upstream.astype(jnp.float32).reshape(FRAMES, ROWS // 2, 2, COLS // 2, 2, CHAN).sum(axis=(2, 4)).astype(jnp.bfloat16)
    units = pooled.reshape(N_TM, FRAME_DEV, N_SPACE, STRIP // 2, COLS // 16, 8 * CHAN)
    units = units.transpose(0, 2, 1, 3, 4, 5).reshape(N_TM, N_SPACE, UNITS, 8 * CHAN)
    owners = owner_map[..., 0]
    one_hot = (owners[..., None] == jnp.arange(N_SPACE, dtype=jnp.int32)).astype(jnp.int32)
    before = jnp.cumsum(one_hot, axis=2)
    position = jnp.sum(before * one_hot, axis=-1) - 1
    slot_index = owners * CAP + position
    placing = (slot_index[..., None, :] == jnp.arange(N_SPACE * CAP, dtype=jnp.int32)[:, None]).astype(jnp.float32)
    outgoing = jnp.einsum("abpu,abuk->abpk", placing, units.astype(jnp.float32), precision=lax.Precision.HIGHEST)
    outgoing = outgoing.astype(jnp.bfloat16).reshape(N_TM, N_SPACE, N_SPACE, CAP, 8 * CHAN)
    return outgoing.transpose(0, 2, 1, 3, 4)
```

```python
import jax
import jax.numpy as jnp
from jax import lax
from jax.experimental import pallas as pl
from jax.experimental.pallas import tpu as pltpu
from jax.sharding import PartitionSpec as P

COLS = 64
C = 128
BF = jnp.bfloat16
F32 = jnp.float32


def side():
    return lax.rem(lax.axis_index("space"), 2)


def shift_add(partial):
    m = partial.shape[0]
    col = lax.broadcasted_iota(jnp.int32, (m, C), 0) % COLS
    low = jnp.where(col == 0, 0.0, pltpu.roll(partial[:, :C], 1, 0))
    high = jnp.where(col == COLS - 1, 0.0, pltpu.roll(partial[:, 2 * C :], m - 1, 0))
    return low + partial[:, C : 2 * C] + high


def patches(ext, t, r0, nr):
    return jnp.concatenate(
        [
            ext[t + dt, r0 + dr : r0 + dr + nr].reshape(nr * COLS, C)
            for dt in range(3)
            for dr in range(3)
        ],
        axis=1,
    )


def conv_back(ext, w, t, r0, nr):
    rhs = jnp.concatenate(
        [
            jnp.concatenate([w[2 - dt, 2 - dr, 2 - j] for j in range(3)], axis=0)
            for dt in range(3)
            for dr in range(3)
        ],
        axis=1,
    )
    out = lax.dot_general(
        patches(ext, t, r0, nr), rhs, (((1,), (1,)), ((), ())), preferred_element_type=F32
    )
    return shift_add(out).reshape(nr, COLS, C)


def conv_fore(ext, w, t, r0, nr):
    rhs = jnp.concatenate(
        [
            jnp.concatenate([w[dt, dr, j] for j in range(3)], axis=1)
            for dt in range(3)
            for dr in range(3)
        ],
        axis=0,
    )
    out = jnp.dot(patches(ext, t, r0, nr), rhs, preferred_element_type=F32)
    return shift_add(out).reshape(nr, COLS, C)


def factor(pre):
    s = jax.nn.sigmoid(pre)
    return s * (1.0 + pre * (1.0 - s))


def put_edges(ext, frames, inner, outer):
    p = side()
    ext[frames, pl.ds(10 * (1 - p), 2)] = inner
    ext[frames, pl.ds(10 * p, 2)] = outer


def store_ten(out, t, value):
    value = value.astype(BF)
    s = lax.axis_index("space")
    zero = jnp.zeros((1, COLS, C), BF)
    out[t, 1:9] = value[1:9]
    out[t, 0:1] = jnp.where(s == 0, zero, value[0:1])
    out[t, 9:10] = jnp.where(s == lax.axis_size("space") - 1, zero, value[9:10])


def send_edges(first, late, rin, rout):
    p = side()
    rin[0:2] = first[:, pl.ds(1 + 6 * (1 - p), 2)]
    rout[0:2] = first[:, pl.ds(1 + 6 * p, 2)]
    rin[2:4] = late[:, pl.ds(6 * (1 - p), 2)]
    rout[2:4] = late[:, pl.ds(6 * p, 2)]


def start_kernel(cot, bi, group, adv, v0, rin, rout, v0s, b1s, b0s, dmi, dmo, dpi, dpo):
    p = side()
    for t in range(4):
        scale = adv[group[t]]
        v0[t] = (cot[t].astype(F32) * scale).astype(BF)
    inner, outer = pl.ds(6 * (1 - p), 2), pl.ds(6 * p, 2)
    rin[0], rout[0] = v0[:, inner], v0[:, outer]
    for k in range(2):
        rin[1 + k], rout[1 + k] = bi[1 - k, :, inner], bi[1 - k, :, outer]
        dpi[k], dpo[k] = bi[1 - k, 2:4, inner], bi[1 - k, 2:4, outer]
    v0s[...] = v0[0:2]
    b1s[...] = bi[1, 2:4]
    b0s[...] = bi[0, 2:4]
    for t in range(2):
        dmi[t] = v0[t, 7 * (1 - p)]
        dmo[t] = v0[t, 7 * p]


def early_kernel(v0, bi, rin, rout, w2, w1, w1n, ga, d1, d0, ext, ext1, ext0):
    ext[:, 2:10] = v0[...]
    put_edges(ext, slice(0, 4), rin[0], rout[0])
    for k, old in enumerate((ext1, ext0)):
        old[:, 2:10] = bi[1 - k]
        put_edges(old, slice(0, 4), rin[1 + k], rout[1 + k])
    for t in range(2):
        ga[t] = conv_back(ext, w2, t, 0, 10)
    for old, w, d in ((ext1, w1, d1), (ext0, w1n, d0)):
        for t in range(2):
            d[t] = factor(conv_fore(old, w, t, 1, 8))


def fore_halo(ext, k, bi, rin, rout, bx, dpi, dpo):
    ext[0:2, 2:10] = bx[...]
    put_edges(ext, slice(0, 2), dpi[k], dpo[k])
    ext[2:4, 2:10] = bi[1 - k, 0:2]
    put_edges(ext, slice(2, 4), rin[1 + k, 0:2], rout[1 + k, 0:2])


def pre01_kernel(bi, rin, rout, bx, dpi, dpo, ga, w1, v1x, ext):
    fore_halo(ext, 0, bi, rin, rout, bx, dpi, dpo)
    for t in range(2):
        store_ten(v1x, t, ga[t] * factor(conv_fore(ext, w1, t, 0, 10)))


def factor01_kernel(bi, rin, rout, bx, dpi, dpo, w1, d, ext):
    fore_halo(ext, 1, bi, rin, rout, bx, dpi, dpo)
    for t in range(2):
        d[t] = factor(conv_fore(ext, w1, t, 0, 10))


def pre23_kernel(v0, rin, rout, vx, dmi, dmo, d, v1x, w2, v1, ein, eout, ext):
    p = side()
    ext[0:2, 2:10] = v0[2:4]
    put_edges(ext, slice(0, 2), rin[0, 2:4], rout[0, 2:4])
    ext[2:4, 2:10] = vx[...]
    for t in range(2):
        ext[2 + t, 10 - 9 * p] = dmi[t]
        ext[2 + t, 1 + 9 * p] = dmo[t]
    for t in range(2):
        v1[t] = (conv_back(ext, w2, t, 1, 8) * d[t]).astype(BF)
    send_edges(v1x, v1, ein, eout)


def local01(ext, vx, v, rin, rout):
    ext[0:2, 1:11] = vx[...]
    ext[2:4, 2:10] = v[...]
    put_edges(ext, slice(0, 4), rin[...], rout[...])


def local23(ext, v, rin, rout, vxr):
    ext[0:2, 2:10] = v[...]
    put_edges(ext, slice(0, 2), rin[2:4], rout[2:4])
    ext[2:4, 1:11] = vxr[...]


def up01_kernel(v1x, v1, rin, rout, v0, r0in, r0out, w1, v2x, ext, old):
    p = side()
    local01(ext, v1x, v1, rin, rout)
    old[:, 2:10] = v0[0:2]
    put_edges(old, slice(0, 2), r0in[0, 0:2], r0out[0, 0:2])
    for t in range(2):
        store_ten(v2x, t, old[t, 1:11].astype(F32) + conv_back(ext, w1, t, 0, 10))


def up23_kernel(v1, rin, rout, vxr, v0, v2x, w1, v2, ein, eout, ext):
    local23(ext, v1, rin, rout, vxr)
    for t in range(2):
        v2[t] = (v0[2 + t].astype(F32) + conv_back(ext, w1, t, 1, 8)).astype(BF)
    send_edges(v2x, v2, ein, eout)


def grad01_kernel(v2x, v2, rin, rout, d, w2, v3x, ext):
    local01(ext, v2x, v2, rin, rout)
    for t in range(2):
        store_ten(v3x, t, conv_back(ext, w2, t, 0, 10) * d[t])


def grad23_kernel(v2, rin, rout, vxr, d, v3x, w2, v3, ein, eout, ext):
    local23(ext, v2, rin, rout, vxr)
    for t in range(2):
        v3[t] = (conv_back(ext, w2, t, 1, 8) * d[t]).astype(BF)
    send_edges(v3x, v3, ein, eout)


def row_pairs(up):
    up = up.astype(BF).astype(F32).reshape(4, 2, COLS, C)
    return up[:, 0] + up[:, 1]


def last01_kernel(v3x, v3, rin, rout, v2x, w1, pool, ext):
    local01(ext, v3x, v3, rin, rout)
    for t in range(2):
        pool[t] = row_pairs(v2x[t, 1:9].astype(F32) + conv_back(ext, w1, t, 1, 8))


def last23_kernel(v3, rin, rout, vxr, v2, pool, owner, w1, out, ext, rows):
    local23(ext, v3, rin, rout, vxr)
    half = 2 * 4 * COLS
    rows[0:half] = pool[...].reshape(half, C)
    for t in range(2):
        pair = row_pairs(v2[t].astype(F32) + conv_back(ext, w1, t, 1, 8))
        rows[half + t * 4 * COLS : half + (t + 1) * 4 * COLS] = pair.reshape(4 * COLS, C)
    units = owner.shape[0]
    slots = out.shape[0]
    capacity = slots // lax.axis_size("space")
    u = lax.broadcasted_iota(jnp.int32, (units, units), 0)
    v = lax.broadcasted_iota(jnp.int32, (units, units), 1)
    mine = jnp.broadcast_to(owner[...], (units, units))
    named = jnp.sum(jnp.where(u == v, mine, 0), axis=0, keepdims=True)
    same = jnp.where((mine == named) & (u < v), 1, 0)
    slot = named * capacity + jnp.sum(same, axis=0, keepdims=True)
    place = jnp.where(
        lax.broadcasted_iota(jnp.int32, (slots, units), 0) == slot, 1.0, 0.0
    ).astype(BF)
    for j in range(8):
        even = rows[pl.ds(2 * j, units, stride=16), :]
        odd = rows[pl.ds(2 * j + 1, units, stride=16), :]
        unit = (even + odd).astype(BF)
        out[:, j * C : (j + 1) * C] = jnp.dot(
            place, unit, preferred_element_type=F32
        ).astype(BF)


VM = pl.BlockSpec(memory_space=pltpu.VMEM)
SM = pl.BlockSpec(memory_space=pltpu.SMEM)


def field(*lead, dtype=BF):
    return jax.ShapeDtypeStruct((*lead, COLS, C), dtype)


def run(kernel, outs, args, units, scratch=None, in_specs=None):
    if scratch is None:
        scratch = [pltpu.VMEM((4, 12, COLS, C), BF)]
    single = not isinstance(outs, list)
    moved = sum(a.size * a.dtype.itemsize for a in args)
    return pl.pallas_call(
        kernel,
        out_shape=outs,
        in_specs=in_specs or [VM] * len(args),
        out_specs=VM if single else [VM] * len(outs),
        scratch_shapes=scratch,
        compiler_params=pltpu.CompilerParams(vmem_limit_bytes=24 << 20),
        cost_estimate=pl.CostEstimate(
            flops=units * COLS * 27 * C * C * 3, bytes_accessed=moved, transcendentals=0
        ),
        name=kernel.__name__,
    )(*args)


def on_device(pixel_cot, frame_group, advantage, block_in, conv1_weight, conv2_weight, owner_map):
    times, strips = lax.axis_size("tm"), lax.axis_size("space")

    def outer_of(s):
        return s + 1 if s % 2 else s - 1

    inner_pairs = [(s, s ^ 1) for s in range(strips)]
    outer_pairs = [(s, outer_of(s)) for s in range(strips) if 0 <= outer_of(s) < strips]
    later = [(t + 1, t) for t in range(times - 1)]
    sooner = [(t, t + 1) for t in range(times - 1)]

    def corner(steps, pairs):
        return [(a * strips + s, b * strips + r) for a, b in steps for s, r in pairs]

    def swap_in(x):
        return lax.ppermute(x, "space", inner_pairs)

    def swap_out(x):
        return lax.ppermute(x, "space", outer_pairs)

    def from_later(x):
        return lax.ppermute(x, "tm", later)

    def both(x, pairs):
        return lax.ppermute(x, ("tm", "space"), pairs)

    w1, w1n = conv1_weight[1], conv1_weight[0]
    w2, w2n = conv2_weight[1], conv2_weight[0]
    bi = block_in
    ext = pltpu.VMEM((4, 12, COLS, C), BF)

    v0, rin, rout, v0s, b1s, b0s, dmi, dmo, dpi, dpo = run(
        start_kernel,
        [
            field(4, 8), field(3, 4, 2), field(3, 4, 2), field(2, 8), field(2, 8), field(2, 8),
            field(2), field(2), field(2, 2, 2), field(2, 2, 2),
        ],
        (pixel_cot, bi, frame_group, advantage),
        1,
        scratch=[],
        in_specs=[VM, VM, SM, SM],
    )
    rin, rout = swap_in(rin), swap_out(rout)
    b1x = lax.ppermute(b1s, "tm", sooner)
    dpi, dpo = both(dpi, corner(sooner, inner_pairs)), both(dpo, corner(sooner, outer_pairs))
    v0x = from_later(v0s)
    dmi, dmo = both(dmi, corner(later, inner_pairs)), both(dmo, corner(later, outer_pairs))
    b0x = lax.ppermute(b0s, "tm", sooner)

    ga, d1, d0 = run(
        early_kernel,
        [field(2, 10, dtype=F32), field(2, 8, dtype=F32), field(2, 8, dtype=F32)],
        (v0, bi, rin, rout, w2, w1, w1n),
        52,
        scratch=[ext, ext, ext],
    )
    v1x = run(pre01_kernel, field(2, 10), (bi, rin, rout, b1x, dpi, dpo, ga, w1), 20)
    v1xr = from_later(v1x)
    edges = [field(2, 8), field(4, 2), field(4, 2)]
    v1, ein, eout = run(pre23_kernel, edges, (v0, rin, rout, v0x, dmi, dmo, d1, v1x, w2), 16)
    r1in, r1out = swap_in(ein), swap_out(eout)
    d0a = run(factor01_kernel, field(2, 10, dtype=F32), (bi, rin, rout, b0x, dpi, dpo, w1n), 20)
    v2x = run(
        up01_kernel,
        field(2, 10),
        (v1x, v1, r1in, r1out, v0, rin, rout, w1),
        20,
        scratch=[ext, pltpu.VMEM((2, 12, COLS, C), BF)],
    )
    v2xr = from_later(v2x)
    v2, ein, eout = run(up23_kernel, edges, (v1, r1in, r1out, v1xr, v0, v2x, w1), 16)
    r2in, r2out = swap_in(ein), swap_out(eout)
    v3x = run(grad01_kernel, field(2, 10), (v2x, v2, r2in, r2out, d0a, w2n), 20)
    v3xr = from_later(v3x)
    v3, ein, eout = run(grad23_kernel, edges, (v2, r2in, r2out, v2xr, d0, v3x, w2n), 16)
    r3in, r3out = swap_in(ein), swap_out(eout)
    pool = run(
        last01_kernel, field(2, 4, dtype=F32), (v3x, v3, r3in, r3out, v2x, w1n), 16
    )
    owner = owner_map.reshape(-1, 1)
    units = owner.shape[0]
    capacity = max(2, 2 * units // strips)
    outgoing = run(
        last23_kernel,
        jax.ShapeDtypeStruct((strips * capacity, 8 * C), BF),
        (v3, r3in, r3out, v3xr, v2, pool, owner, w1n),
        16,
        scratch=[ext, pltpu.VMEM((4 * 4 * COLS, C), F32)],
    )
    outgoing = outgoing.reshape(strips, capacity, 8 * C)
    arrived = lax.all_to_all(outgoing, "space", split_axis=0, concat_axis=0, tiled=True)
    return arrived.reshape(1, 1, strips, capacity, 8 * C)


def solution(mesh):
    in_specs = (
        P("tm", "space", None, None),
        P("tm"),
        P(),
        P(None, "tm", "space", None, None),
        P(),
        P(),
        P("tm", "space", None, None),
    )
    out_specs = P("tm", "space", None, None, None)
    return jax.shard_map(
        on_device, mesh=mesh, in_specs=in_specs, out_specs=out_specs, check_vma=False
    )
```

```python
import jax
import jax.numpy as jnp
from jax import lax
from jax.experimental import pallas as pl
from jax.experimental.pallas import tpu as pltpu
from jax.sharding import PartitionSpec as P

COLS = 64
C = 128
BF = jnp.bfloat16
F32 = jnp.float32


def side():
    return lax.rem(lax.axis_index("space"), 2)


def shift_add(partial):
    m = partial.shape[0]
    col = lax.broadcasted_iota(jnp.int32, (m, C), 0) % COLS
    low = jnp.where(col == 0, 0.0, pltpu.roll(partial[:, :C], 1, 0))
    high = jnp.where(col == COLS - 1, 0.0, pltpu.roll(partial[:, 2 * C :], m - 1, 0))
    return low + partial[:, C : 2 * C] + high


def patches(ext, t, r0, nr, steps=(0, 1, 2)):
    return jnp.concatenate(
        [
            ext[t + dt, r0 + dr : r0 + dr + nr].reshape(nr * COLS, C)
            for dt in steps
            for dr in range(3)
        ],
        axis=1,
    )


def conv_back(ext, w, layer, t, r0, nr, steps=(0, 1, 2)):
    rhs = jnp.concatenate(
        [
            jnp.concatenate([w[layer, 2 - dt, 2 - dr, 2 - j] for j in range(3)], axis=0)
            for dt in steps
            for dr in range(3)
        ],
        axis=1,
    )
    out = lax.dot_general(
        patches(ext, t, r0, nr, steps),
        rhs,
        (((1,), (1,)), ((), ())),
        preferred_element_type=F32,
    )
    return shift_add(out).reshape(nr, COLS, C)


def conv_fore(ext, w, layer, t, r0, nr):
    rhs = jnp.concatenate(
        [
            jnp.concatenate([w[layer, dt, dr, j] for j in range(3)], axis=1)
            for dt in range(3)
            for dr in range(3)
        ],
        axis=0,
    )
    out = jnp.dot(patches(ext, t, r0, nr), rhs, preferred_element_type=F32)
    return shift_add(out).reshape(nr, COLS, C)


def factor(pre):
    s = jax.nn.sigmoid(pre)
    return s * (1.0 + pre * (1.0 - s))


def inside(outer):
    s = lax.axis_index("space")
    end = (s == 0) | (s == lax.axis_size("space") - 1)
    return jnp.where(end, jnp.zeros_like(outer), outer)


def with_later(halo):
    last = lax.axis_index("tm") == lax.axis_size("tm") - 1
    return jnp.where(last, jnp.zeros_like(halo), halo)


def with_sooner(halo):
    return jnp.where(lax.axis_index("tm") == 0, jnp.zeros_like(halo), halo)


def put_edges(ext, frames, inner, outer):
    p = side()
    ext[frames, pl.ds(10 * (1 - p), 2)] = inner
    ext[frames, pl.ds(10 * p, 2)] = inside(outer)


def store_ten(out, t, value):
    value = value.astype(BF)
    s = lax.axis_index("space")
    zero = jnp.zeros((1, COLS, C), BF)
    out[t, 1:9] = value[1:9]
    out[t, 0:1] = jnp.where(s == 0, zero, value[0:1])
    out[t, 9:10] = jnp.where(s == lax.axis_size("space") - 1, zero, value[9:10])


def send_edges(first, late, rin, rout):
    p = side()
    rin[0:2] = first[:, pl.ds(1 + 6 * (1 - p), 2)]
    rout[0:2] = first[:, pl.ds(1 + 6 * p, 2)]
    rin[2:4] = late[:, pl.ds(6 * (1 - p), 2)]
    rout[2:4] = late[:, pl.ds(6 * p, 2)]


def start_kernel(cot, bi, group, adv, v0, rin, rout, raw, gs, ads, sem):
    p = side()
    inner, outer = pl.ds(6 * (1 - p), 2), pl.ds(6 * p, 2)
    copies = [
        pltpu.make_async_copy(group, gs, sem.at[0]),
        pltpu.make_async_copy(adv, ads, sem.at[1]),
    ]
    copies += [pltpu.make_async_copy(cot.at[t], raw.at[t], sem.at[2 + t]) for t in range(4)]
    for k in range(2):
        copies += [
            pltpu.make_async_copy(bi.at[1 - k, :, inner], rin.at[1 + k], sem.at[6 + 2 * k]),
            pltpu.make_async_copy(bi.at[1 - k, :, outer], rout.at[1 + k], sem.at[7 + 2 * k]),
        ]
    for copy in copies:
        copy.start()
    copies[0].wait()
    copies[1].wait()
    for t in range(4):
        copies[2 + t].wait()
        scale = ads[gs[t]]
        v0[t] = (raw[t].astype(F32) * scale).astype(BF)
        rin[0, t] = (raw[t, inner].astype(F32) * scale).astype(BF)
        rout[0, t] = (raw[t, outer].astype(F32) * scale).astype(BF)
    for copy in copies[6:]:
        copy.wait()


def extend_kernel(v0, bi, rin, rout, vx, bx):
    p = side()
    for t in range(2):
        vx[t, 1:9] = v0[t]
        vx[t, 9 * (1 - p)] = rin[0, t, p]
        vx[t, 9 * p] = inside(rout[0, t, 1 - p])
    bx[:, 2:10] = bi[1, 2:4]
    put_edges(bx, slice(0, 2), rin[1, 2:4], rout[1, 2:4])


def early_kernel(v0, bi, rin, rout, w2, w1h, ga, d1, d0, bx, ext, ext1, ext0, w1, sem):
    weights = pltpu.make_async_copy(w1h, w1, sem)
    weights.start()
    ext[:, 2:10] = v0[...]
    put_edges(ext, slice(0, 4), rin[0], rout[0])
    for k, old in enumerate((ext1, ext0)):
        old[:, 2:10] = bi[1 - k]
        put_edges(old, slice(0, 4), rin[1 + k], rout[1 + k])
    bx[...] = ext0[2:4]
    for t in range(2):
        ga[t] = conv_back(ext, w2, 1, t, 0, 10)
    weights.wait()
    for k, (old, d) in enumerate(((ext1, d1), (ext0, d0))):
        for t in range(2):
            d[t] = factor(conv_fore(old, w1, 1 - k, t, 1, 8))


def fore_halo(ext, k, bi, rin, rout, bx):
    ext[0:2] = with_sooner(bx[...])
    ext[2:4, 2:10] = bi[1 - k, 0:2]
    put_edges(ext, slice(2, 4), rin[1 + k, 0:2], rout[1 + k, 0:2])


def pre01_kernel(bi, rin, rout, bx, ga, w1, v1x, ext):
    fore_halo(ext, 0, bi, rin, rout, bx)
    for t in range(2):
        store_ten(v1x, t, ga[t] * factor(conv_fore(ext, w1, 1, t, 0, 10)))


def factor01_kernel(bi, rin, rout, bx, w1, d, ext):
    fore_halo(ext, 1, bi, rin, rout, bx)
    for t in range(2):
        d[t] = factor(conv_fore(ext, w1, 0, t, 0, 10))


def pre23_kernel(v0, rin, rout, vx, d, v1x, w2, v1, ein, eout, ext):
    ext[0:2, 2:10] = v0[2:4]
    put_edges(ext, slice(0, 2), rin[0, 2:4], rout[0, 2:4])
    ext[2:4, 1:11] = with_later(vx[...])
    for t in range(2):
        v1[t] = (conv_back(ext, w2, 1, t, 1, 8) * d[t]).astype(BF)
    send_edges(v1x, v1, ein, eout)


def local01(ext, vx, v, rin, rout):
    ext[0:2, 1:11] = vx[...]
    ext[2:4, 2:10] = v[...]
    put_edges(ext, slice(0, 4), rin[...], rout[...])


def local23(ext, v, rin, rout, vxr):
    ext[0:2, 2:10] = v[...]
    put_edges(ext, slice(0, 2), rin[2:4], rout[2:4])
    ext[2:4, 1:11] = with_later(vxr[...])


def up01_kernel(v1x, v1, rin, rout, v0, r0in, r0out, w1, v2x, ext, old):
    p = side()
    local01(ext, v1x, v1, rin, rout)
    old[:, 2:10] = v0[0:2]
    put_edges(old, slice(0, 2), r0in[0, 0:2], r0out[0, 0:2])
    for t in range(2):
        store_ten(v2x, t, old[t, 1:11].astype(F32) + conv_back(ext, w1, 1, t, 0, 10))


def up23_kernel(v1, rin, rout, vxr, v0, v2x, w1, v2, ein, eout, ext):
    local23(ext, v1, rin, rout, vxr)
    for t in range(2):
        v2[t] = (v0[2 + t].astype(F32) + conv_back(ext, w1, 1, t, 1, 8)).astype(BF)
    send_edges(v2x, v2, ein, eout)


def grad01_kernel(v2x, v2, rin, rout, d, w2, v3x, ext):
    local01(ext, v2x, v2, rin, rout)
    for t in range(2):
        store_ten(v3x, t, conv_back(ext, w2, 0, t, 0, 10) * d[t])


def grad23_kernel(v2, rin, rout, vxr, d, v3x, w2, v3, ein, eout, ext):
    local23(ext, v2, rin, rout, vxr)
    for t in range(2):
        v3[t] = (conv_back(ext, w2, 0, t, 1, 8) * d[t]).astype(BF)
    send_edges(v3x, v3, ein, eout)


def row_pairs(up):
    up = up.astype(BF).astype(F32).reshape(4, 2, COLS, C)
    return up[:, 0] + up[:, 1]


def last01_kernel(v3x, v3, rin, rout, v2x, v2, w1, pool, part, ext):
    local01(ext, v3x, v3, rin, rout)
    for t in range(2):
        pool[t] = row_pairs(v2x[t, 1:9].astype(F32) + conv_back(ext, w1, 0, t, 1, 8))
    for t, steps in ((0, (0, 1)), (1, (0,))):
        part[t] = v2[t].astype(F32) + conv_back(ext, w1, 0, 2 + t, 1, 8, steps)


def last23_kernel(vxr, pool, part, owner, w1, out, ext, rows):
    ext[2:4, 1:11] = with_later(vxr[...])
    half = 2 * 4 * COLS
    rows[0:half] = pool[...].reshape(half, C)
    for t, steps in ((0, (2,)), (1, (1, 2))):
        pair = row_pairs(part[t] + conv_back(ext, w1, 0, t, 1, 8, steps))
        rows[half + t * 4 * COLS : half + (t + 1) * 4 * COLS] = pair.reshape(4 * COLS, C)
    units = owner.shape[0]
    strips, capacity = out.shape[0], out.shape[1]
    slots = strips * capacity
    u = lax.broadcasted_iota(jnp.int32, (units, units), 0)
    v = lax.broadcasted_iota(jnp.int32, (units, units), 1)
    mine = jnp.broadcast_to(owner[...], (units, units))
    named = jnp.sum(jnp.where(u == v, mine, 0), axis=0, keepdims=True)
    same = jnp.where((mine == named) & (u < v), 1, 0)
    slot = named * capacity + jnp.sum(same, axis=0, keepdims=True)
    place = jnp.where(
        lax.broadcasted_iota(jnp.int32, (slots, units), 0) == slot, 1.0, 0.0
    ).astype(BF)
    for j in range(8):
        even = rows[pl.ds(2 * j, units, stride=16), :]
        odd = rows[pl.ds(2 * j + 1, units, stride=16), :]
        unit = (even + odd).astype(BF)
        sent = jnp.dot(place, unit, preferred_element_type=F32)
        out[:, :, j * C : (j + 1) * C] = sent.reshape(strips, capacity, C).astype(BF)


VM = pl.BlockSpec(memory_space=pltpu.VMEM)
SM = pl.BlockSpec(memory_space=pltpu.SMEM)


def field(*lead, dtype=BF):
    return jax.ShapeDtypeStruct((*lead, COLS, C), dtype)


def run(kernel, outs, args, units, scratch=None, in_specs=None):
    if scratch is None:
        scratch = [pltpu.VMEM((4, 12, COLS, C), BF)]
    single = not isinstance(outs, list)
    moved = sum(a.size * a.dtype.itemsize for a in args)
    return pl.pallas_call(
        kernel,
        out_shape=outs,
        in_specs=in_specs or [VM] * len(args),
        out_specs=VM if single else [VM] * len(outs),
        scratch_shapes=scratch,
        compiler_params=pltpu.CompilerParams(vmem_limit_bytes=40 << 20),
        cost_estimate=pl.CostEstimate(
            flops=units * COLS * 27 * C * C * 3, bytes_accessed=moved, transcendentals=0
        ),
        name=kernel.__name__,
    )(*args)


def in_hbm(x):
    return pltpu.with_memory_space_constraint(x, pltpu.HBM)


def on_device(pixel_cot, frame_group, advantage, block_in, conv1_weight, conv2_weight, owner_map):
    times, strips = lax.axis_size("tm"), lax.axis_size("space")

    inner_pairs = [(s, s ^ 1) for s in range(strips)]
    outer_pairs = [(s, (s + 1 if s % 2 else s - 1) % strips) for s in range(strips)]
    later = [((t + 1) % times, t) for t in range(times)]
    sooner = [(t, (t + 1) % times) for t in range(times)]

    def swap_in(x):
        return lax.ppermute(x, "space", inner_pairs)

    def swap_out(x):
        return lax.ppermute(x, "space", outer_pairs)

    def from_later(x):
        return lax.ppermute(x, "tm", later)

    def from_sooner(x):
        return lax.ppermute(x, "tm", sooner)

    w1, w2 = conv1_weight, conv2_weight
    bi = block_in
    ext = pltpu.VMEM((4, 12, COLS, C), BF)

    v0, rin, rout = run(
        start_kernel,
        [field(4, 8), field(3, 4, 2), field(3, 4, 2)],
        tuple(in_hbm(x) for x in (pixel_cot, bi, frame_group, advantage)),
        1,
        scratch=[
            pltpu.VMEM((4, 8, COLS, C), BF),
            pltpu.SMEM(frame_group.shape, jnp.int32),
            pltpu.SMEM(advantage.shape, F32),
            pltpu.SemaphoreType.DMA((10,)),
        ],
        in_specs=[pl.BlockSpec(memory_space=pltpu.HBM)] * 4,
    )
    rin, rout = swap_in(rin), swap_out(rout)
    v0x, b1x = run(extend_kernel, [field(2, 10), field(2, 12)], (v0, bi, rin, rout), 1, scratch=[])
    b1x = from_sooner(b1x)
    v0x = from_later(v0x)
    ga, d1, d0, b0x = run(
        early_kernel,
        [field(2, 10, dtype=F32), field(2, 8, dtype=F32), field(2, 8, dtype=F32), field(2, 12)],
        (v0, bi, rin, rout, w2, in_hbm(w1)),
        52,
        scratch=[ext, ext, ext, pltpu.VMEM(w1.shape, BF), pltpu.SemaphoreType.DMA],
        in_specs=[VM] * 5 + [pl.BlockSpec(memory_space=pltpu.HBM)],
    )
    b0x = from_sooner(b0x)
    v1x = run(pre01_kernel, field(2, 10), (bi, rin, rout, b1x, ga, w1), 20)
    v1xr = from_later(v1x)
    edges = [field(2, 8), field(4, 2), field(4, 2)]
    v1, ein, eout = run(pre23_kernel, edges, (v0, rin, rout, v0x, d1, v1x, w2), 16)
    r1in, r1out = swap_in(ein), swap_out(eout)
    d0a = run(factor01_kernel, field(2, 10, dtype=F32), (bi, rin, rout, b0x, w1), 20)
    v2x = run(
        up01_kernel,
        field(2, 10),
        (v1x, v1, r1in, r1out, v0, rin, rout, w1),
        20,
        scratch=[ext, pltpu.VMEM((2, 12, COLS, C), BF)],
    )
    v2xr = from_later(v2x)
    v2, ein, eout = run(up23_kernel, edges, (v1, r1in, r1out, v1xr, v0, v2x, w1), 16)
    r2in, r2out = swap_in(ein), swap_out(eout)
    v3x = run(grad01_kernel, field(2, 10), (v2x, v2, r2in, r2out, d0a, w2), 20)
    v3xr = from_later(v3x)
    v3, ein, eout = run(grad23_kernel, edges, (v2, r2in, r2out, v2xr, d0, v3x, w2), 16)
    r3in, r3out = swap_in(ein), swap_out(eout)
    pool, part = run(
        last01_kernel,
        [field(2, 4, dtype=F32), field(2, 8, dtype=F32)],
        (v3x, v3, r3in, r3out, v2x, v2, w1),
        24,
    )
    owner = owner_map.reshape(-1, 1)
    units = owner.shape[0]
    capacity = max(2, 2 * units // strips)
    outgoing = run(
        last23_kernel,
        jax.ShapeDtypeStruct((strips, capacity, 8 * C), BF),
        (v3xr, pool, part, owner, w1),
        8,
        scratch=[ext, pltpu.VMEM((4 * 4 * COLS, C), F32)],
    )
    arrived = lax.all_to_all(outgoing, "space", split_axis=0, concat_axis=0, tiled=True)
    return arrived.reshape(1, 1, strips, capacity, 8 * C)


def solution(mesh):
    in_specs = (
        P("tm", "space", None, None),
        P("tm"),
        P(),
        P(None, "tm", "space", None, None),
        P(),
        P(),
        P("tm", "space", None, None),
    )
    out_specs = P("tm", "space", None, None, None)
    return jax.shard_map(
        on_device, mesh=mesh, in_specs=in_specs, out_specs=out_specs, check_vma=False
    )
```

```python
import jax
import jax.numpy as jnp
from jax import lax
from jax.experimental import pallas as pl
from jax.experimental.pallas import tpu as pltpu
from jax.sharding import PartitionSpec as P

COLS = 64
C = 128
BF = jnp.bfloat16
F32 = jnp.float32


def side():
    return lax.rem(lax.axis_index("space"), 2)


def shift_add(partial):
    m = partial.shape[0]
    col = lax.broadcasted_iota(jnp.int32, (m, C), 0) % COLS
    low = jnp.where(col == 0, 0.0, pltpu.roll(partial[:, :C], 1, 0))
    high = jnp.where(col == COLS - 1, 0.0, pltpu.roll(partial[:, 2 * C :], m - 1, 0))
    return low + partial[:, C : 2 * C] + high


def patches(ext, t, r0, nr, steps=(0, 1, 2)):
    return jnp.concatenate(
        [
            ext[t + dt, r0 + dr : r0 + dr + nr].reshape(nr * COLS, C)
            for dt in steps
            for dr in range(3)
        ],
        axis=1,
    )


def back_taps(lhs, w, layer, steps=(0, 1, 2)):
    rhs = jnp.concatenate(
        [
            jnp.concatenate([w[layer, 2 - dt, 2 - dr, 2 - j] for j in range(3)], axis=0)
            for dt in steps
            for dr in range(3)
        ],
        axis=1,
    )
    return shift_add(
        lax.dot_general(lhs, rhs, (((1,), (1,)), ((), ())), preferred_element_type=F32)
    )


def conv_back(ext, w, layer, t, r0, nr, steps=(0, 1, 2)):
    return back_taps(patches(ext, t, r0, nr, steps), w, layer, steps).reshape(nr, COLS, C)


def conv_fore(ext, w, layer, t, r0, nr, steps=(0, 1, 2)):
    rhs = jnp.concatenate(
        [
            jnp.concatenate([w[layer, dt, dr, j] for j in range(3)], axis=1)
            for dt in steps
            for dr in range(3)
        ],
        axis=0,
    )
    out = jnp.dot(patches(ext, t, r0, nr, steps), rhs, preferred_element_type=F32)
    return shift_add(out).reshape(nr, COLS, C)


def factor(pre):
    s = jax.nn.sigmoid(pre)
    return s * (1.0 + pre * (1.0 - s))


def inside(outer):
    s = lax.axis_index("space")
    end = (s == 0) | (s == lax.axis_size("space") - 1)
    return jnp.where(end, jnp.zeros_like(outer), outer)


def with_later(halo):
    last = lax.axis_index("tm") == lax.axis_size("tm") - 1
    return jnp.where(last, jnp.zeros_like(halo), halo)


def with_sooner(halo):
    return jnp.where(lax.axis_index("tm") == 0, jnp.zeros_like(halo), halo)


def put_edges(ext, frames, inner, outer):
    p = side()
    ext[frames, pl.ds(10 * (1 - p), 2)] = inner
    ext[frames, pl.ds(10 * p, 2)] = inside(outer)


def store_ten(out, t, value):
    value = value.astype(BF)
    s = lax.axis_index("space")
    zero = jnp.zeros((1, COLS, C), BF)
    out[t, 1:9] = value[1:9]
    out[t, 0:1] = jnp.where(s == 0, zero, value[0:1])
    out[t, 9:10] = jnp.where(s == lax.axis_size("space") - 1, zero, value[9:10])


def send_edges(first, late, rin, rout):
    p = side()
    rin[0:2] = first[:, pl.ds(1 + 6 * (1 - p), 2)]
    rout[0:2] = first[:, pl.ds(1 + 6 * p, 2)]
    rin[2:4] = late[:, pl.ds(6 * (1 - p), 2)]
    rout[2:4] = late[:, pl.ds(6 * p, 2)]


def start_kernel(
    cot, bi, group, adv, v0, rin, rout, b1s, dpi, dpo, raw, gs, ads, sem
):
    p = side()
    inner, outer = pl.ds(6 * (1 - p), 2), pl.ds(6 * p, 2)
    copies = [
        pltpu.make_async_copy(group, gs, sem.at[0]),
        pltpu.make_async_copy(adv, ads, sem.at[1]),
    ]
    copies += [pltpu.make_async_copy(cot.at[t], raw.at[t], sem.at[2 + t]) for t in range(4)]
    copies += [
        pltpu.make_async_copy(bi.at[1, pl.ds(2, 2)], b1s, sem.at[6]),
        pltpu.make_async_copy(bi.at[1, :, inner], rin.at[1], sem.at[7]),
        pltpu.make_async_copy(bi.at[1, :, outer], rout.at[1], sem.at[8]),
        pltpu.make_async_copy(bi.at[1, pl.ds(2, 2), inner], dpi, sem.at[9]),
        pltpu.make_async_copy(bi.at[1, pl.ds(2, 2), outer], dpo, sem.at[10]),
        pltpu.make_async_copy(bi.at[0, :, inner], rin.at[2], sem.at[11]),
        pltpu.make_async_copy(bi.at[0, :, outer], rout.at[2], sem.at[12]),
    ]
    for copy in copies:
        copy.start()
    copies[0].wait()
    copies[1].wait()
    for t in range(4):
        copies[2 + t].wait()
        scale = ads[gs[t]]
        v0[t] = (raw[t].astype(F32) * scale).astype(BF)
        rin[0, t] = (raw[t, inner].astype(F32) * scale).astype(BF)
        rout[0, t] = (raw[t, outer].astype(F32) * scale).astype(BF)
    for copy in copies[6:]:
        copy.wait()


def extend_kernel(v0, rin, rout, vx):
    p = side()
    for t in range(2):
        vx[t, 1:9] = v0[t]
        vx[t, 9 * (1 - p)] = rin[0, t, p]
        vx[t, 9 * p] = inside(rout[0, t, 1 - p])


def extend0_kernel(bi, rin, rout, after, bx):
    bx[:, 2:10] = bi[0, 2:4]
    put_edges(bx, slice(0, 2), rin[2, 2:4], rout[2, 2:4])


def early_kernel(v0, bih, rin, rout, w2h, w1h, ga, ga23, d1, pre, ext, ext1, w2, w1, sem):
    copies = [
        pltpu.make_async_copy(w2h.at[1], w2.at[1], sem.at[0]),
        pltpu.make_async_copy(bih.at[1], ext1.at[:, pl.ds(2, 8)], sem.at[1]),
        pltpu.make_async_copy(w1h.at[1], w1.at[1], sem.at[2]),
    ]
    for copy in copies:
        copy.start()
    ext[:, 2:10] = v0[...]
    put_edges(ext, slice(0, 4), rin[0], rout[0])
    copies[0].wait()
    for t in range(2):
        ga[t] = conv_back(ext, w2, 1, t, 0, 10)
    for t, steps in ((0, (0, 1)), (1, (0,))):
        ga23[t] = conv_back(ext, w2, 1, 2 + t, 1, 8, steps)
    copies[1].wait()
    copies[2].wait()
    put_edges(ext1, slice(0, 4), rin[1], rout[1])
    for t in range(2):
        d1[t] = factor(conv_fore(ext1, w1, 1, t, 1, 8))
    for t, steps in ((0, (2,)), (1, (1, 2))):
        pre[t] = conv_fore(ext1, w1, 1, t - 2, 0, 10, steps)


def pre01_kernel(bx, dpi, dpo, ga, pre, w1, v1x, ext):
    ext[:, 2:10] = with_sooner(bx[...])
    put_edges(ext, slice(0, 2), with_sooner(dpi[...]), with_sooner(dpo[...]))
    for t, steps in ((0, (0, 1)), (1, (0,))):
        whole = pre[t] + conv_fore(ext, w1, 1, t, 0, 10, steps)
        store_ten(v1x, t, ga[t] * factor(whole))


def factor_kernel(bi, rin, rout, bx, after, w1, da, d, ext):
    ext[0:2] = with_sooner(bx[...])
    ext[2:6, 2:10] = bi[0]
    put_edges(ext, slice(2, 6), rin[2], rout[2])
    for t in range(2):
        da[t] = factor(conv_fore(ext, w1, 0, t, 0, 10))
    for t in range(2):
        d[t] = factor(conv_fore(ext, w1, 0, 2 + t, 1, 8))


def later_part(ext, w, layer):
    return [
        conv_back(ext, w, layer, t, 1, 8, steps) for t, steps in ((0, (2,)), (1, (1, 2)))
    ]


def pre23_kernel(ga23, vx, d, v1x, w2, v1, ein, eout, ext):
    ext[2:4, 1:11] = with_later(vx[...])
    for t, more in enumerate(later_part(ext, w2, 1)):
        v1[t] = ((ga23[t] + more) * d[t]).astype(BF)
    send_edges(v1x, v1, ein, eout)


def local01(ext, vx, v, rin, rout):
    ext[0:2, 1:11] = vx[...]
    ext[2:4, 2:10] = v[...]
    put_edges(ext, slice(0, 4), rin[...], rout[...])


def local23(ext, v, rin, rout, vxr):
    ext[0:2, 2:10] = v[...]
    put_edges(ext, slice(0, 2), rin[2:4], rout[2:4])
    ext[2:4, 1:11] = with_later(vxr[...])


def up01_kernel(v1x, v1, rin, rout, v0, r0in, r0out, w1, v2x, ext, old):
    p = side()
    local01(ext, v1x, v1, rin, rout)
    old[:, 2:10] = v0[0:2]
    put_edges(old, slice(0, 2), r0in[0, 0:2], r0out[0, 0:2])
    for t in range(2):
        store_ten(v2x, t, old[t, 1:11].astype(F32) + conv_back(ext, w1, 1, t, 0, 10))


def grad01_kernel(v2x, v2, rin, rout, d, w2, v3x, ext):
    local01(ext, v2x, v2, rin, rout)
    for t in range(2):
        store_ten(v3x, t, conv_back(ext, w2, 0, t, 0, 10) * d[t])


def up23_kernel(v1, rin, rout, vxr, v0, v2x, w1, v2, ein, eout, ext):
    local23(ext, v1, rin, rout, vxr)
    for t in range(2):
        v2[t] = (v0[2 + t].astype(F32) + conv_back(ext, w1, 1, t, 1, 8)).astype(BF)
    send_edges(v2x, v2, ein, eout)


def grad23_kernel(v2, rin, rout, vxr, d, v3x, w2, v3, ein, eout, ext):
    local23(ext, v2, rin, rout, vxr)
    for t in range(2):
        v3[t] = (conv_back(ext, w2, 0, t, 1, 8) * d[t]).astype(BF)
    p = side()
    for t in range(2):
        ein[t], eout[t] = v3x[t, 1 + 7 * (1 - p)], v3x[t, 1 + 7 * p]
        ein[2 + t], eout[2 + t] = v3[t, 7 * (1 - p)], v3[t, 7 * p]


def row_pairs(up):
    up = up.astype(BF).astype(F32).reshape(4, 2, COLS, C)
    return up[:, 0] + up[:, 1]


def last01_kernel(v3x, v3, rin, rout, v2x, v2, w1, pool, part, ext):
    p = side()
    ext[0:2, 1:11] = v3x[...]
    ext[2:4, 2:10] = v3[...]
    for t in range(4):
        ext[t, 10 - 9 * p] = rin[t]
        ext[t, 1 + 9 * p] = inside(rout[t])
    for t in range(2):
        pool[t] = row_pairs(v2x[t, 1:9].astype(F32) + conv_back(ext, w1, 0, t, 1, 8))
    for t, steps in ((0, (0, 1)), (1, (0,))):
        part[t] = v2[t].astype(F32) + conv_back(ext, w1, 0, 2 + t, 1, 8, steps)


def last23_kernel(vxr, pool, part, owner, w1, out, ext, rows):
    ext[2:4, 1:11] = with_later(vxr[...])
    half = 2 * 4 * COLS
    rows[0:half] = pool[...].reshape(half, C)
    for t, more in enumerate(later_part(ext, w1, 0)):
        pair = row_pairs(part[t] + more)
        rows[half + t * 4 * COLS : half + (t + 1) * 4 * COLS] = pair.reshape(4 * COLS, C)
    units = owner.shape[1]
    strips, capacity = out.shape[0], out.shape[1]
    slots = strips * capacity
    u = lax.broadcasted_iota(jnp.int32, (units, units), 0)
    v = lax.broadcasted_iota(jnp.int32, (units, units), 1)
    named = owner[...]
    mine = jnp.sum(jnp.where(u == v, jnp.broadcast_to(named, (units, units)), 0), axis=1, keepdims=True)
    same = jnp.where((mine == named) & (u < v), 1, 0)
    slot = named * capacity + jnp.sum(same, axis=0, keepdims=True)
    place = jnp.where(
        lax.broadcasted_iota(jnp.int32, (slots, units), 0) == slot, 1.0, 0.0
    ).astype(BF)
    for j in range(8):
        even = rows[pl.ds(2 * j, units, stride=16), :]
        odd = rows[pl.ds(2 * j + 1, units, stride=16), :]
        unit = (even + odd).astype(BF)
        sent = jnp.dot(place, unit, preferred_element_type=F32)
        out[:, :, j * C : (j + 1) * C] = sent.reshape(strips, capacity, C).astype(BF)


VM = pl.BlockSpec(memory_space=pltpu.VMEM)
HB = pl.BlockSpec(memory_space=pltpu.HBM)


def field(*lead, dtype=BF):
    return jax.ShapeDtypeStruct((*lead, COLS, C), dtype)


def run(kernel, outs, args, units, scratch=None, in_specs=None):
    if scratch is None:
        scratch = [pltpu.VMEM((4, 12, COLS, C), BF)]
    single = not isinstance(outs, list)
    moved = sum(a.size * a.dtype.itemsize for a in args)
    return pl.pallas_call(
        kernel,
        out_shape=outs,
        in_specs=in_specs or [VM] * len(args),
        out_specs=VM if single else [VM] * len(outs),
        scratch_shapes=scratch,
        compiler_params=pltpu.CompilerParams(vmem_limit_bytes=40 << 20),
        cost_estimate=pl.CostEstimate(
            flops=units * COLS * 27 * C * C * 2, bytes_accessed=moved, transcendentals=0
        ),
        name=kernel.__name__,
    )(*args)


def in_hbm(x):
    return pltpu.with_memory_space_constraint(x, pltpu.HBM)


def on_device(pixel_cot, frame_group, advantage, block_in, conv1_weight, conv2_weight, owner_map):
    times, strips = lax.axis_size("tm"), lax.axis_size("space")

    inner_pairs = [(s, s ^ 1) for s in range(strips)]
    outer_pairs = [(s, (s + 1 if s % 2 else s - 1) % strips) for s in range(strips)]
    later = [((t + 1) % times, t) for t in range(times)]
    sooner = [(t, (t + 1) % times) for t in range(times)]

    def swap_in(x):
        return lax.ppermute(x, "space", inner_pairs)

    def swap_out(x):
        return lax.ppermute(x, "space", outer_pairs)

    def from_later(x):
        return lax.ppermute(x, "tm", later)

    def corner(x, steps, pairs):
        route = [(a * strips + s, b * strips + r) for a, b in steps for s, r in pairs]
        return lax.ppermute(x, ("tm", "space"), route)

    def from_sooner(x):
        return lax.ppermute(x, "tm", sooner)

    w1, w2 = conv1_weight, conv2_weight
    bi = block_in
    ext = pltpu.VMEM((4, 12, COLS, C), BF)

    ten, eight = field(2, 10, dtype=F32), field(2, 8, dtype=F32)
    edges = [field(2, 8), field(4, 2), field(4, 2)]

    v0, rin, rout, b1x, dpi, dpo = run(
        start_kernel,
        [
            field(4, 8), field(3, 4, 2), field(3, 4, 2), field(2, 8), field(2, 2), field(2, 2),
        ],
        tuple(in_hbm(x) for x in (pixel_cot, bi, frame_group, advantage)),
        1,
        scratch=[
            pltpu.VMEM((4, 8, COLS, C), BF),
            pltpu.SMEM(frame_group.shape, jnp.int32),
            pltpu.SMEM(advantage.shape, F32),
            pltpu.SemaphoreType.DMA((13,)),
        ],
        in_specs=[HB] * 4,
    )
    b1x = from_sooner(b1x)
    rout, rin = swap_out(rout), swap_in(rin)
    dpo, dpi = corner(dpo, sooner, outer_pairs), corner(dpi, sooner, inner_pairs)
    v0x = from_later(run(extend_kernel, field(2, 10), (v0, rin, rout), 1, scratch=[]))
    ga, ga23, d1, pre = run(
        early_kernel,
        [ten, eight, eight, ten],
        (v0, in_hbm(bi), rin, rout, in_hbm(w2), in_hbm(w1)),
        54,
        scratch=[
            ext,
            ext,
            pltpu.VMEM(w2.shape, BF),
            pltpu.VMEM(w1.shape, BF),
            pltpu.SemaphoreType.DMA((3,)),
        ],
        in_specs=[VM, HB, VM, VM, HB, HB],
    )
    v1x = run(
        pre01_kernel,
        field(2, 10),
        (b1x, dpi, dpo, ga, pre, w1),
        10,
        scratch=[pltpu.VMEM((2, 12, COLS, C), BF)],
    )
    v1xr = from_later(v1x)
    v1, ein, eout = run(pre23_kernel, edges, (ga23, v0x, d1, v1x, w2), 8)
    r1out, r1in = swap_out(eout), swap_in(ein)
    b0x = run(extend0_kernel, field(2, 12), (bi, rin, rout, v1), 1, scratch=[])
    b0x = from_sooner(b0x)
    v2x = run(
        up01_kernel,
        field(2, 10),
        (v1x, v1, r1in, r1out, v0, rin, rout, w1),
        20,
        scratch=[ext, pltpu.VMEM((2, 12, COLS, C), BF)],
    )
    v2xr = from_later(v2x)
    v2, ein, eout = run(up23_kernel, edges, (v1, r1in, r1out, v1xr, v0, v2x, w1), 16)
    r2out, r2in = swap_out(eout), swap_in(ein)
    d0a, d0 = run(
        factor_kernel,
        [ten, eight],
        (bi, rin, rout, b0x, v2, w1),
        36,
        scratch=[pltpu.VMEM((6, 12, COLS, C), BF)],
    )
    v3x = run(grad01_kernel, field(2, 10), (v2x, v2, r2in, r2out, d0a, w2), 20)
    v3xr = from_later(v3x)
    v3, ein, eout = run(grad23_kernel, [field(2, 8), field(4), field(4)], (v2, r2in, r2out, v2xr, d0, v3x, w2), 16)
    r3out, r3in = swap_out(eout), swap_in(ein)
    pool, part = run(
        last01_kernel,
        [field(2, 4, dtype=F32), eight],
        (v3x, v3, r3in, r3out, v2x, v2, w1),
        24,
    )
    owner = owner_map.reshape(1, -1)
    units = owner.shape[1]
    capacity = max(2, 2 * units // strips)
    outgoing = run(
        last23_kernel,
        jax.ShapeDtypeStruct((strips, capacity, 8 * C), BF),
        (v3xr, pool, part, owner, w1),
        8,
        scratch=[ext, pltpu.VMEM((4 * 4 * COLS, C), F32)],
    )
    arrived = lax.all_to_all(outgoing, "space", split_axis=0, concat_axis=0, tiled=True)
    return arrived.reshape(1, 1, strips, capacity, 8 * C)


def solution(mesh):
    in_specs = (
        P("tm", "space", None, None),
        P("tm"),
        P(),
        P(None, "tm", "space", None, None),
        P(),
        P(),
        P("tm", "space", None, None),
    )
    out_specs = P("tm", "space", None, None, None)
    return jax.shard_map(
        on_device, mesh=mesh, in_specs=in_specs, out_specs=out_specs, check_vma=False
    )
```

```python
import jax
import jax.numpy as jnp
from jax import lax
from jax.experimental import pallas as pl
from jax.experimental.pallas import tpu as pltpu
from jax.sharding import PartitionSpec as P

COLS = 64
C = 128
BF = jnp.bfloat16
F32 = jnp.float32


def side():
    return lax.rem(lax.axis_index("space"), 2)


def shift_add(partial):
    m = partial.shape[0]
    col = lax.broadcasted_iota(jnp.int32, (m, C), 0) % COLS
    low = jnp.where(col == 0, 0.0, pltpu.roll(partial[:, :C], 1, 0))
    high = jnp.where(col == COLS - 1, 0.0, pltpu.roll(partial[:, 2 * C :], m - 1, 0))
    return low + partial[:, C : 2 * C] + high


def patches(ext, t, r0, nr, steps=(0, 1, 2)):
    return jnp.concatenate(
        [
            ext[t + dt, r0 + dr : r0 + dr + nr].reshape(nr * COLS, C)
            for dt in steps
            for dr in range(3)
        ],
        axis=1,
    )


def back_taps(lhs, w, layer, steps=(0, 1, 2)):
    rhs = jnp.concatenate(
        [
            jnp.concatenate([w[layer, 2 - dt, 2 - dr, 2 - j] for j in range(3)], axis=0)
            for dt in steps
            for dr in range(3)
        ],
        axis=1,
    )
    return shift_add(
        lax.dot_general(lhs, rhs, (((1,), (1,)), ((), ())), preferred_element_type=F32)
    )


def conv_back(ext, w, layer, t, r0, nr, steps=(0, 1, 2)):
    return back_taps(patches(ext, t, r0, nr, steps), w, layer, steps).reshape(nr, COLS, C)


def conv_fore(ext, w, layer, t, r0, nr, steps=(0, 1, 2)):
    rhs = jnp.concatenate(
        [
            jnp.concatenate([w[layer, dt, dr, j] for j in range(3)], axis=1)
            for dt in steps
            for dr in range(3)
        ],
        axis=0,
    )
    out = jnp.dot(patches(ext, t, r0, nr, steps), rhs, preferred_element_type=F32)
    return shift_add(out).reshape(nr, COLS, C)


def factor(pre):
    s = jax.nn.sigmoid(pre)
    return s * (1.0 + pre * (1.0 - s))


def inside(outer):
    s = lax.axis_index("space")
    end = (s == 0) | (s == lax.axis_size("space") - 1)
    return jnp.where(end, jnp.zeros_like(outer), outer)


def with_later(halo):
    last = lax.axis_index("tm") == lax.axis_size("tm") - 1
    return jnp.where(last, jnp.zeros_like(halo), halo)


def with_sooner(halo):
    return jnp.where(lax.axis_index("tm") == 0, jnp.zeros_like(halo), halo)


def put_edges(ext, frames, inner, outer):
    p = side()
    ext[frames, pl.ds(10 * (1 - p), 2)] = inner
    ext[frames, pl.ds(10 * p, 2)] = inside(outer)


def store_ten(out, t, value):
    value = value.astype(BF)
    s = lax.axis_index("space")
    zero = jnp.zeros((1, COLS, C), BF)
    out[t, 1:9] = value[1:9]
    out[t, 0:1] = jnp.where(s == 0, zero, value[0:1])
    out[t, 9:10] = jnp.where(s == lax.axis_size("space") - 1, zero, value[9:10])


def send_edges(first, late, rin, rout):
    p = side()
    rin[0:2] = first[:, pl.ds(1 + 6 * (1 - p), 2)]
    rout[0:2] = first[:, pl.ds(1 + 6 * p, 2)]
    rin[2:4] = late[:, pl.ds(6 * (1 - p), 2)]
    rout[2:4] = late[:, pl.ds(6 * p, 2)]


def start_kernel(
    cot, bi, group, adv, v0, rin, rout, b1s, dpi, dpo, raw, gs, ads, sem
):
    p = side()
    inner, outer = pl.ds(6 * (1 - p), 2), pl.ds(6 * p, 2)
    copies = [
        pltpu.make_async_copy(group, gs, sem.at[0]),
        pltpu.make_async_copy(adv, ads, sem.at[1]),
    ]
    copies += [pltpu.make_async_copy(cot.at[t], raw.at[t], sem.at[2 + t]) for t in range(4)]
    copies += [
        pltpu.make_async_copy(bi.at[1, pl.ds(2, 2)], b1s, sem.at[6]),
        pltpu.make_async_copy(bi.at[1, :, inner], rin.at[1], sem.at[7]),
        pltpu.make_async_copy(bi.at[1, :, outer], rout.at[1], sem.at[8]),
        pltpu.make_async_copy(bi.at[1, pl.ds(2, 2), inner], dpi, sem.at[9]),
        pltpu.make_async_copy(bi.at[1, pl.ds(2, 2), outer], dpo, sem.at[10]),
        pltpu.make_async_copy(bi.at[0, :, inner], rin.at[2], sem.at[11]),
        pltpu.make_async_copy(bi.at[0, :, outer], rout.at[2], sem.at[12]),
    ]
    for copy in copies:
        copy.start()
    copies[0].wait()
    copies[1].wait()
    for t in range(4):
        copies[2 + t].wait()
        scale = ads[gs[t]]
        v0[t] = (raw[t].astype(F32) * scale).astype(BF)
        rin[0, t] = (raw[t, inner].astype(F32) * scale).astype(BF)
        rout[0, t] = (raw[t, outer].astype(F32) * scale).astype(BF)
    for copy in copies[6:]:
        copy.wait()


def extend_kernel(v0, rin, rout, vx):
    p = side()
    for t in range(2):
        vx[t, 1:9] = v0[t]
        vx[t, 9 * (1 - p)] = rin[0, t, p]
        vx[t, 9 * p] = inside(rout[0, t, 1 - p])


def extend0_kernel(bi, rin, rout, after, bx):
    bx[:, 2:10] = bi[0, 2:4]
    put_edges(bx, slice(0, 2), rin[2, 2:4], rout[2, 2:4])


def fetch_kernel(after, bi, w2, w1, bi1, w2o, w1o, sem):
    copies = [
        pltpu.make_async_copy(w2.at[pl.ds(1, 1)], w2o, sem.at[0]),
        pltpu.make_async_copy(w1.at[pl.ds(1, 1)], w1o, sem.at[1]),
        pltpu.make_async_copy(bi.at[1], bi1, sem.at[2]),
    ]
    for copy in copies:
        copy.start()
    for copy in copies:
        copy.wait()


def early_kernel(v0, bi1, rin, rout, w2, w1, ga, ga23, d1, pre, ext, ext1):
    ext[:, 2:10] = v0[...]
    put_edges(ext, slice(0, 4), rin[0], rout[0])
    for t in range(2):
        ga[t] = conv_back(ext, w2, 0, t, 0, 10)
    for t, steps in ((0, (0, 1)), (1, (0,))):
        ga23[t] = conv_back(ext, w2, 0, 2 + t, 1, 8, steps)
    ext1[:, 2:10] = bi1[...]
    put_edges(ext1, slice(0, 4), rin[1], rout[1])
    for t in range(2):
        d1[t] = factor(conv_fore(ext1, w1, 0, t, 1, 8))
    for t, steps in ((0, (2,)), (1, (1, 2))):
        pre[t] = conv_fore(ext1, w1, 0, t - 2, 0, 10, steps)


def pre01_kernel(bx, dpi, dpo, ga, pre, w1, v1x, ext):
    ext[:, 2:10] = with_sooner(bx[...])
    put_edges(ext, slice(0, 2), with_sooner(dpi[...]), with_sooner(dpo[...]))
    for t, steps in ((0, (0, 1)), (1, (0,))):
        whole = pre[t] + conv_fore(ext, w1, 1, t, 0, 10, steps)
        store_ten(v1x, t, ga[t] * factor(whole))


def factor_kernel(bi, rin, rout, bx, after, w1, da, d, ext):
    ext[0:2] = with_sooner(bx[...])
    ext[2:6, 2:10] = bi[0]
    put_edges(ext, slice(2, 6), rin[2], rout[2])
    for t in range(2):
        da[t] = factor(conv_fore(ext, w1, 0, t, 0, 10))
    for t in range(2):
        d[t] = factor(conv_fore(ext, w1, 0, 2 + t, 1, 8))


def later_part(ext, w, layer):
    return [
        conv_back(ext, w, layer, t, 1, 8, steps) for t, steps in ((0, (2,)), (1, (1, 2)))
    ]


def pre23_kernel(ga23, vx, d, v1x, w2, v1, ein, eout, ext):
    ext[2:4, 1:11] = with_later(vx[...])
    for t, more in enumerate(later_part(ext, w2, 1)):
        v1[t] = ((ga23[t] + more) * d[t]).astype(BF)
    send_edges(v1x, v1, ein, eout)


def local01(ext, vx, v, rin, rout):
    ext[0:2, 1:11] = vx[...]
    ext[2:4, 2:10] = v[...]
    put_edges(ext, slice(0, 4), rin[...], rout[...])


def local23(ext, v, rin, rout, vxr):
    ext[0:2, 2:10] = v[...]
    put_edges(ext, slice(0, 2), rin[2:4], rout[2:4])
    ext[2:4, 1:11] = with_later(vxr[...])


def up01_kernel(v1x, v1, rin, rout, v0, r0in, r0out, w1, v2x, ext, old):
    p = side()
    local01(ext, v1x, v1, rin, rout)
    old[:, 2:10] = v0[0:2]
    put_edges(old, slice(0, 2), r0in[0, 0:2], r0out[0, 0:2])
    for t in range(2):
        store_ten(v2x, t, old[t, 1:11].astype(F32) + conv_back(ext, w1, 1, t, 0, 10))


def grad01_kernel(v2x, v2, rin, rout, d, w2, v3x, ext):
    local01(ext, v2x, v2, rin, rout)
    for t in range(2):
        store_ten(v3x, t, conv_back(ext, w2, 0, t, 0, 10) * d[t])


def up23_kernel(v1, rin, rout, vxr, v0, v2x, w1, v2, ein, eout, ext):
    local23(ext, v1, rin, rout, vxr)
    for t in range(2):
        v2[t] = (v0[2 + t].astype(F32) + conv_back(ext, w1, 1, t, 1, 8)).astype(BF)
    send_edges(v2x, v2, ein, eout)


def grad23_kernel(v2, rin, rout, vxr, d, v3x, w2, v3, ein, eout, ext):
    local23(ext, v2, rin, rout, vxr)
    for t in range(2):
        v3[t] = (conv_back(ext, w2, 0, t, 1, 8) * d[t]).astype(BF)
    p = side()
    for t in range(2):
        ein[t], eout[t] = v3[t, 7 * (1 - p)], v3[t, 7 * p]


def row_pairs(up):
    up = up.astype(BF).astype(F32).reshape(4, 2, COLS, C)
    return up[:, 0] + up[:, 1]


def inner_last_kernel(v3x, v3, v2x, v2, w1, base, ext):
    ext[0:2, 1:11] = v3x[...]
    ext[2:4, 2:10] = v3[...]
    ext[2:4, 1:2] = jnp.zeros((2, 1, COLS, C), BF)
    ext[2:4, 10:11] = jnp.zeros((2, 1, COLS, C), BF)
    for t in range(2):
        base[t] = v2x[t, 1:9].astype(F32) + conv_back(ext, w1, 0, t, 1, 8)
    for t, steps in ((0, (0, 1)), (1, (0,))):
        base[2 + t] = v2[t].astype(F32) + conv_back(ext, w1, 0, 2 + t, 1, 8, steps)


def edge_rows(halo, w, layer, dr):
    zero = jnp.zeros((COLS, C), BF)
    frames = [zero, zero, halo[0], halo[1], zero, zero]
    lhs = [jnp.concatenate(frames[t : t + 3], axis=1) for t in range(4)]
    rhs = [
        jnp.concatenate([w[layer, 2 - dt, 2 - dr, 2 - j] for j in range(3)], axis=0)
        for dt in range(3)
    ]
    out = lax.dot_general(
        jnp.concatenate(lhs, axis=0),
        jnp.concatenate(rhs, axis=1),
        (((1,), (1,)), ((), ())),
        preferred_element_type=F32,
    )
    return shift_add(out).reshape(4, 1, COLS, C)


def last_kernel(base, rin, rout, vxr, owner, w1, out, ext, rows):
    ext[2:4, 1:11] = with_later(vxr[...])
    low, near = side() == 1, rin[...]
    far = inside(rout[...])
    top = edge_rows(jnp.where(low, near, far), w1, 0, 0)
    bottom = edge_rows(jnp.where(low, far, near), w1, 0, 2)
    more = [0.0, 0.0, *later_part(ext, w1, 0)]
    for t in range(4):
        whole = jnp.concatenate(
            [base[t, 0:1] + top[t], base[t, 1:7], base[t, 7:8] + bottom[t]], axis=0
        )
        pair = row_pairs(whole + more[t])
        rows[t * 4 * COLS : (t + 1) * 4 * COLS] = pair.reshape(4 * COLS, C)
    units = owner.shape[1]
    strips, capacity = out.shape[0], out.shape[1]
    slots = strips * capacity
    u = lax.broadcasted_iota(jnp.int32, (units, units), 0)
    v = lax.broadcasted_iota(jnp.int32, (units, units), 1)
    named = owner[...]
    mine = jnp.sum(jnp.where(u == v, jnp.broadcast_to(named, (units, units)), 0), axis=1, keepdims=True)
    same = jnp.where((mine == named) & (u < v), 1, 0)
    slot = named * capacity + jnp.sum(same, axis=0, keepdims=True)
    place = jnp.where(
        lax.broadcasted_iota(jnp.int32, (slots, units), 0) == slot, 1.0, 0.0
    ).astype(BF)
    for j in range(8):
        even = rows[pl.ds(2 * j, units, stride=16), :]
        odd = rows[pl.ds(2 * j + 1, units, stride=16), :]
        unit = (even + odd).astype(BF)
        sent = jnp.dot(place, unit, preferred_element_type=F32)
        out[:, :, j * C : (j + 1) * C] = sent.reshape(strips, capacity, C).astype(BF)


VM = pl.BlockSpec(memory_space=pltpu.VMEM)
HB = pl.BlockSpec(memory_space=pltpu.HBM)


def field(*lead, dtype=BF):
    return jax.ShapeDtypeStruct((*lead, COLS, C), dtype)


def run(kernel, outs, args, units, scratch=None, in_specs=None):
    if scratch is None:
        scratch = [pltpu.VMEM((4, 12, COLS, C), BF)]
    single = not isinstance(outs, list)
    moved = sum(a.size * a.dtype.itemsize for a in args)
    return pl.pallas_call(
        kernel,
        out_shape=outs,
        in_specs=in_specs or [VM] * len(args),
        out_specs=VM if single else [VM] * len(outs),
        scratch_shapes=scratch,
        compiler_params=pltpu.CompilerParams(vmem_limit_bytes=40 << 20),
        cost_estimate=pl.CostEstimate(
            flops=units * COLS * 27 * C * C * 2, bytes_accessed=moved, transcendentals=0
        ),
        name=kernel.__name__,
    )(*args)


def in_hbm(x):
    return pltpu.with_memory_space_constraint(x, pltpu.HBM)


def on_device(pixel_cot, frame_group, advantage, block_in, conv1_weight, conv2_weight, owner_map):
    times, strips = lax.axis_size("tm"), lax.axis_size("space")

    inner_pairs = [(s, s ^ 1) for s in range(strips)]
    outer_pairs = [(s, (s + 1 if s % 2 else s - 1) % strips) for s in range(strips)]
    later = [((t + 1) % times, t) for t in range(times)]
    sooner = [(t, (t + 1) % times) for t in range(times)]

    def swap_in(x):
        return lax.ppermute(x, "space", inner_pairs)

    def swap_out(x):
        return lax.ppermute(x, "space", outer_pairs)

    def from_later(x):
        return lax.ppermute(x, "tm", later)

    def corner(x, steps, pairs):
        route = [(a * strips + s, b * strips + r) for a, b in steps for s, r in pairs]
        return lax.ppermute(x, ("tm", "space"), route)

    def from_sooner(x):
        return lax.ppermute(x, "tm", sooner)

    w1, w2 = conv1_weight, conv2_weight
    bi = block_in
    ext = pltpu.VMEM((4, 12, COLS, C), BF)

    ten, eight = field(2, 10, dtype=F32), field(2, 8, dtype=F32)
    edges = [field(2, 8), field(4, 2), field(4, 2)]

    v0, rin, rout, b1x, dpi, dpo = run(
        start_kernel,
        [
            field(4, 8), field(3, 4, 2), field(3, 4, 2), field(2, 8), field(2, 2), field(2, 2),
        ],
        tuple(in_hbm(x) for x in (pixel_cot, bi, frame_group, advantage)),
        1,
        scratch=[
            pltpu.VMEM((4, 8, COLS, C), BF),
            pltpu.SMEM(frame_group.shape, jnp.int32),
            pltpu.SMEM(advantage.shape, F32),
            pltpu.SemaphoreType.DMA((13,)),
        ],
        in_specs=[HB] * 4,
    )
    b1x = from_sooner(b1x)
    rout, rin = swap_out(rout), swap_in(rin)
    dpo, dpi = corner(dpo, sooner, outer_pairs), corner(dpi, sooner, inner_pairs)
    v0x = from_later(run(extend_kernel, field(2, 10), (v0, rin, rout), 1, scratch=[]))
    taps = jax.ShapeDtypeStruct((1, *w1.shape[1:]), BF)
    bi1, w2late, w1late = run(
        fetch_kernel,
        [field(4, 8), taps, taps],
        (v0, in_hbm(bi), in_hbm(w2), in_hbm(w1)),
        1,
        scratch=[pltpu.SemaphoreType.DMA((3,))],
        in_specs=[VM, HB, HB, HB],
    )
    ga, ga23, d1, pre = run(
        early_kernel,
        [ten, eight, eight, ten],
        (v0, bi1, rin, rout, w2late, w1late),
        54,
        scratch=[ext, ext],
    )
    v1x = run(
        pre01_kernel,
        field(2, 10),
        (b1x, dpi, dpo, ga, pre, w1),
        10,
        scratch=[pltpu.VMEM((2, 12, COLS, C), BF)],
    )
    v1xr = from_later(v1x)
    v1, ein, eout = run(pre23_kernel, edges, (ga23, v0x, d1, v1x, w2), 8)
    r1out, r1in = swap_out(eout), swap_in(ein)
    b0x = run(extend0_kernel, field(2, 12), (bi, rin, rout, v1), 1, scratch=[])
    b0x = from_sooner(b0x)
    v2x = run(
        up01_kernel,
        field(2, 10),
        (v1x, v1, r1in, r1out, v0, rin, rout, w1),
        20,
        scratch=[ext, pltpu.VMEM((2, 12, COLS, C), BF)],
    )
    v2xr = from_later(v2x)
    v2, ein, eout = run(up23_kernel, edges, (v1, r1in, r1out, v1xr, v0, v2x, w1), 16)
    r2out, r2in = swap_out(eout), swap_in(ein)
    d0a, d0 = run(
        factor_kernel,
        [ten, eight],
        (bi, rin, rout, b0x, v2, w1),
        36,
        scratch=[pltpu.VMEM((6, 12, COLS, C), BF)],
    )
    v3x = run(grad01_kernel, field(2, 10), (v2x, v2, r2in, r2out, d0a, w2), 20)
    v3xr = from_later(v3x)
    v3, ein, eout = run(grad23_kernel, [field(2, 8), field(2), field(2)], (v2, r2in, r2out, v2xr, d0, v3x, w2), 16)
    r3out, r3in = swap_out(eout), swap_in(ein)
    base = run(inner_last_kernel, field(4, 8, dtype=F32), (v3x, v3, v2x, v2, w1), 24)
    owner = owner_map.reshape(1, -1)
    units = owner.shape[1]
    capacity = max(2, 2 * units // strips)
    outgoing = run(
        last_kernel,
        jax.ShapeDtypeStruct((strips, capacity, 8 * C), BF),
        (base, r3in, r3out, v3xr, owner, w1),
        8,
        scratch=[ext, pltpu.VMEM((4 * 4 * COLS, C), F32)],
    )
    arrived = lax.all_to_all(outgoing, "space", split_axis=0, concat_axis=0, tiled=True)
    return arrived.reshape(1, 1, strips, capacity, 8 * C)


def solution(mesh):
    in_specs = (
        P("tm", "space", None, None),
        P("tm"),
        P(),
        P(None, "tm", "space", None, None),
        P(),
        P(),
        P("tm", "space", None, None),
    )
    out_specs = P("tm", "space", None, None, None)
    return jax.shard_map(
        on_device, mesh=mesh, in_specs=in_specs, out_specs=out_specs, check_vma=False
    )
```

```python
import jax
import jax.numpy as jnp
from jax import lax
from jax.experimental import pallas as pl
from jax.experimental.pallas import tpu as pltpu
from jax.sharding import PartitionSpec as P

COLS = 64
C = 128
BF = jnp.bfloat16
F32 = jnp.float32


def side():
    return lax.rem(lax.axis_index("space"), 2)


def shift_add(partial):
    m = partial.shape[0]
    col = lax.broadcasted_iota(jnp.int32, (m, C), 0) % COLS
    low = jnp.where(col == 0, 0.0, pltpu.roll(partial[:, :C], 1, 0))
    high = jnp.where(col == COLS - 1, 0.0, pltpu.roll(partial[:, 2 * C :], m - 1, 0))
    return low + partial[:, C : 2 * C] + high


def patches(ext, t, r0, nr, steps=(0, 1, 2)):
    return jnp.concatenate(
        [
            ext[t + dt, r0 + dr : r0 + dr + nr].reshape(nr * COLS, C)
            for dt in steps
            for dr in range(3)
        ],
        axis=1,
    )


def back_taps(lhs, w, layer, steps=(0, 1, 2), rows=(0, 1, 2)):
    rhs = jnp.concatenate(
        [
            jnp.concatenate([w[layer, 2 - dt, 2 - dr, 2 - j] for j in range(3)], axis=0)
            for dt in steps
            for dr in rows
        ],
        axis=1,
    )
    return shift_add(
        lax.dot_general(lhs, rhs, (((1,), (1,)), ((), ())), preferred_element_type=F32)
    )


def conv_back(ext, w, layer, t, r0, nr, steps=(0, 1, 2)):
    return back_taps(patches(ext, t, r0, nr, steps), w, layer, steps).reshape(nr, COLS, C)


def conv_fore(ext, w, layer, t, r0, nr, steps=(0, 1, 2)):
    rhs = jnp.concatenate(
        [
            jnp.concatenate([w[layer, dt, dr, j] for j in range(3)], axis=1)
            for dt in steps
            for dr in range(3)
        ],
        axis=0,
    )
    out = jnp.dot(patches(ext, t, r0, nr, steps), rhs, preferred_element_type=F32)
    return shift_add(out).reshape(nr, COLS, C)


def factor(pre):
    s = jax.nn.sigmoid(pre)
    return s * (1.0 + pre * (1.0 - s))


def inside(outer):
    s = lax.axis_index("space")
    end = (s == 0) | (s == lax.axis_size("space") - 1)
    return jnp.where(end, jnp.zeros_like(outer), outer)


def with_later(halo):
    last = lax.axis_index("tm") == lax.axis_size("tm") - 1
    return jnp.where(last, jnp.zeros_like(halo), halo)


def with_sooner(halo):
    return jnp.where(lax.axis_index("tm") == 0, jnp.zeros_like(halo), halo)


def put_edges(ext, frames, inner, outer):
    p = side()
    ext[frames, pl.ds(10 * (1 - p), 2)] = inner
    ext[frames, pl.ds(10 * p, 2)] = inside(outer)


def store_ten(out, t, value):
    value = value.astype(BF)
    s = lax.axis_index("space")
    zero = jnp.zeros((1, COLS, C), BF)
    out[t, 1:9] = value[1:9]
    out[t, 0:1] = jnp.where(s == 0, zero, value[0:1])
    out[t, 9:10] = jnp.where(s == lax.axis_size("space") - 1, zero, value[9:10])


def send_edges(first, late, ein, eout):
    p = side()
    for t in range(2):
        ein[t], eout[t] = first[t, 7 - 5 * p], first[t, 2 + 5 * p]
        for k in range(2):
            ein[2 + 2 * t + k] = late[t, 6 * (1 - p) + k]
            eout[2 + 2 * t + k] = late[t, 6 * p + k]


def start_kernel(
    cot, bi, group, adv, v0, rin, rout, b1s, dpi, dpo, raw, gs, ads, sem
):
    p = side()
    inner, outer = pl.ds(6 * (1 - p), 2), pl.ds(6 * p, 2)
    copies = [
        pltpu.make_async_copy(group, gs, sem.at[0]),
        pltpu.make_async_copy(adv, ads, sem.at[1]),
    ]
    copies += [pltpu.make_async_copy(cot.at[t], raw.at[t], sem.at[2 + t]) for t in range(4)]
    copies += [
        pltpu.make_async_copy(bi.at[1, pl.ds(2, 2)], b1s, sem.at[6]),
        pltpu.make_async_copy(bi.at[1, :, inner], rin.at[1], sem.at[7]),
        pltpu.make_async_copy(bi.at[1, :, outer], rout.at[1], sem.at[8]),
        pltpu.make_async_copy(bi.at[1, pl.ds(2, 2), inner], dpi, sem.at[9]),
        pltpu.make_async_copy(bi.at[1, pl.ds(2, 2), outer], dpo, sem.at[10]),
        pltpu.make_async_copy(bi.at[0, :, inner], rin.at[2], sem.at[11]),
        pltpu.make_async_copy(bi.at[0, :, outer], rout.at[2], sem.at[12]),
    ]
    for copy in copies:
        copy.start()
    copies[0].wait()
    copies[1].wait()
    for t in range(4):
        copies[2 + t].wait()
        scale = ads[gs[t]]
        v0[t] = (raw[t].astype(F32) * scale).astype(BF)
        rin[0, t] = (raw[t, inner].astype(F32) * scale).astype(BF)
        rout[0, t] = (raw[t, outer].astype(F32) * scale).astype(BF)
    for copy in copies[6:]:
        copy.wait()


def extend_kernel(v0, rin, rout, vx):
    p = side()
    for t in range(2):
        vx[t, 1:9] = v0[t]
        vx[t, 9 * (1 - p)] = rin[0, t, p]
        vx[t, 9 * p] = inside(rout[0, t, 1 - p])


def extend0_kernel(bi, rin, rout, after, bx):
    bx[:, 2:10] = bi[0, 2:4]
    put_edges(bx, slice(0, 2), rin[2, 2:4], rout[2, 2:4])


def fetch_kernel(after, bi, w2, w1, bi1, w2o, w1o, sem):
    copies = [
        pltpu.make_async_copy(w2.at[pl.ds(1, 1)], w2o, sem.at[0]),
        pltpu.make_async_copy(w1.at[pl.ds(1, 1)], w1o, sem.at[1]),
        pltpu.make_async_copy(bi.at[1], bi1, sem.at[2]),
    ]
    for copy in copies:
        copy.start()
    for copy in copies:
        copy.wait()


def early_kernel(v0, bi1, rin, rout, w2, w1, ga, ga23, d1, pre, ext, ext1):
    ext[:, 2:10] = v0[...]
    put_edges(ext, slice(0, 4), rin[0], rout[0])
    for t in range(2):
        ga[t] = conv_back(ext, w2, 0, t, 0, 10)
    for t, steps in ((0, (0, 1)), (1, (0,))):
        ga23[t] = conv_back(ext, w2, 0, 2 + t, 1, 8, steps)
    ext1[:, 2:10] = bi1[...]
    put_edges(ext1, slice(0, 4), rin[1], rout[1])
    for t in range(2):
        d1[t] = factor(conv_fore(ext1, w1, 0, t, 1, 8))
    for t, steps in ((0, (2,)), (1, (1, 2))):
        pre[t] = conv_fore(ext1, w1, 0, t - 2, 0, 10, steps)


def pre01_kernel(bx, dpi, dpo, ga, pre, w1, v1x, ext):
    ext[:, 2:10] = with_sooner(bx[...])
    put_edges(ext, slice(0, 2), with_sooner(dpi[...]), with_sooner(dpo[...]))
    for t, steps in ((0, (0, 1)), (1, (0,))):
        whole = pre[t] + conv_fore(ext, w1, 1, t, 0, 10, steps)
        store_ten(v1x, t, ga[t] * factor(whole))


def factor01_kernel(bi, rin, rout, bx, after, w1, d, ext):
    ext[0:2] = with_sooner(bx[...])
    ext[2:4, 2:10] = bi[0, 0:2]
    put_edges(ext, slice(2, 4), rin[2, 0:2], rout[2, 0:2])
    for t in range(2):
        d[t] = factor(conv_fore(ext, w1, 0, t, 0, 10))


def factor23_kernel(bi, rin, rout, after, w1, d, ext):
    ext[:, 2:10] = bi[0]
    put_edges(ext, slice(0, 4), rin[2], rout[2])
    for t in range(2):
        d[t] = factor(conv_fore(ext, w1, 0, t, 1, 8))


def later_part(ext, w, layer):
    return [
        conv_back(ext, w, layer, t, 1, 8, steps) for t, steps in ((0, (2,)), (1, (1, 2)))
    ]


def pre23_kernel(ga23, vx, d, v1x, w2, v1, ein, eout, ext):
    ext[2:4, 1:11] = with_later(vx[...])
    for t, more in enumerate(later_part(ext, w2, 1)):
        v1[t] = ((ga23[t] + more) * d[t]).astype(BF)
    send_edges(v1x, v1, ein, eout)


def up01_kernel(base01, rin, rout, w1, v2x):
    top, bottom = rim_rows(*halos(rin, rout), w1, 1)
    for t in range(2):
        store_ten(v2x, t, ten_rows(base01, t, top, bottom))


def grad01_kernel(base01, rin, rout, d, after, w2, v3x):
    top, bottom = rim_rows(*halos(rin, rout), w2, 0)
    for t in range(2):
        store_ten(v3x, t, ten_rows(base01, t, top, bottom) * d[t])


def whole23(base23, rin, rout, vxr, w, layer, ext):
    ext[2:4, 1:11] = with_later(vxr[...])
    above, below = halos(rin, rout)
    top = edge_rows([above[3], above[5]], w, layer, 0, 2)
    bottom = edge_rows([below[2], below[4]], w, layer, 2, 2)
    more = later_part(ext, w, layer)
    return [eight_rows(base23, t, top, bottom) + more[t] for t in range(2)]


def up23_kernel(base23, rin, rout, vxr, v2x, w1, v2, ein, eout, ext):
    for t, whole in enumerate(whole23(base23, rin, rout, vxr, w1, 1, ext)):
        v2[t] = whole.astype(BF)
    send_edges(v2x, v2, ein, eout)


def grad23_kernel(base23, rin, rout, vxr, d, w2, v3, ein, eout, ext):
    for t, whole in enumerate(whole23(base23, rin, rout, vxr, w2, 0, ext)):
        v3[t] = (whole * d[t]).astype(BF)
    p = side()
    for t in range(2):
        ein[t], eout[t] = v3[t, 7 * (1 - p)], v3[t, 7 * p]


def row_pairs(up):
    up = up.astype(BF).astype(F32).reshape(4, 2, COLS, C)
    return up[:, 0] + up[:, 1]


def inner_last_kernel(v3x, v3, v2x, v2, w1, base, ext):
    ext[0:2, 1:11] = v3x[...]
    ext[2:4, 2:10] = v3[...]
    ext[2:4, 1:2] = jnp.zeros((2, 1, COLS, C), BF)
    ext[2:4, 10:11] = jnp.zeros((2, 1, COLS, C), BF)
    for t in range(2):
        base[t] = v2x[t, 1:9].astype(F32) + conv_back(ext, w1, 0, t, 1, 8)
    for t, steps in ((0, (0, 1)), (1, (0,))):
        base[2 + t] = v2[t].astype(F32) + conv_back(ext, w1, 0, 2 + t, 1, 8, steps)


def edge_rows(halo, w, layer, dr, first=0):
    zero = jnp.zeros((COLS, C), BF)
    frames = [zero, zero, halo[0], halo[1], zero, zero]
    lhs = [jnp.concatenate(frames[t : t + 3], axis=1) for t in range(first, 4)]
    out = back_taps(jnp.concatenate(lhs, axis=0), w, layer, rows=(dr,))
    return out.reshape(4 - first, 1, COLS, C)


def halos(rin, rout):
    low, near, far = side() == 1, rin[...], inside(rout[...])
    return jnp.where(low, near, far), jnp.where(low, far, near)


def rim_rows(above, below, w, layer):
    zero = jnp.zeros((COLS, C), BF)
    up = [(above[0], zero), (above[1], zero), (above[2], above[3]), (above[4], above[5])]
    down = [(zero, below[0]), (zero, below[1]), (below[2], below[3]), (below[4], below[5])]
    tops, bottoms = [], []
    for t in range(2):
        three = range(t, t + 3)
        tops += [
            [x for f in three for x in up[f]],
            [x for f in three for x in (up[f][1], zero)],
        ]
        bottoms += [
            [x for f in three for x in (zero, down[f][0])],
            [x for f in three for x in down[f]],
        ]
    out = []
    for lines, rows in ((tops, (0, 1)), (bottoms, (1, 2))):
        lhs = jnp.concatenate([jnp.concatenate(line, axis=1) for line in lines], axis=0)
        out.append(back_taps(lhs, w, layer, rows=rows).reshape(2, 2, COLS, C))
    return out


def local_part(ext, vx, v, w, layer):
    ext[0:2, 1:11] = vx[...]
    ext[2:4, 2:10] = v[...]
    for frames, edge in ((slice(0, 2), 1), (slice(2, 4), 2)):
        ext[frames, 0:edge] = jnp.zeros((2, edge, COLS, C), BF)
        ext[frames, 12 - edge : 12] = jnp.zeros((2, edge, COLS, C), BF)
    first = [conv_back(ext, w, layer, t, 0, 10) for t in range(2)]
    late = [
        conv_back(ext, w, layer, 2 + t, 1, 8, steps) for t, steps in ((0, (0, 1)), (1, (0,)))
    ]
    return first, late


def inner_up_kernel(v1x, v1, v0, r0in, r0out, w1, base01, base23, ext, old):
    old[:, 2:10] = v0[0:2]
    put_edges(old, slice(0, 2), r0in[0, 0:2], r0out[0, 0:2])
    first, late = local_part(ext, v1x, v1, w1, 1)
    for t in range(2):
        base01[t] = old[t, 1:11].astype(F32) + first[t]
        base23[t] = v0[2 + t].astype(F32) + late[t]


def inner_grad_kernel(v2x, v2, after, w2, base01, base23, ext):
    first, late = local_part(ext, v2x, v2, w2, 0)
    for t in range(2):
        base01[t], base23[t] = first[t], late[t]


def ten_rows(base, t, top, bottom):
    return jnp.concatenate(
        [base[t, 0:2] + top[t], base[t, 2:8], base[t, 8:10] + bottom[t]], axis=0
    )


def eight_rows(base, t, top, bottom):
    return jnp.concatenate(
        [base[t, 0:1] + top[t], base[t, 1:7], base[t, 7:8] + bottom[t]], axis=0
    )


def last_kernel(base, rin, rout, vxr, owner, w1, out, ext, rows):
    ext[2:4, 1:11] = with_later(vxr[...])
    above, below = halos(rin, rout)
    top, bottom = edge_rows(above, w1, 0, 0), edge_rows(below, w1, 0, 2)
    more = [0.0, 0.0, *later_part(ext, w1, 0)]
    for t in range(4):
        pair = row_pairs(eight_rows(base, t, top, bottom) + more[t])
        rows[t * 4 * COLS : (t + 1) * 4 * COLS] = pair.reshape(4 * COLS, C)
    units = owner.shape[1]
    strips, capacity = out.shape[0], out.shape[1]
    slots = strips * capacity
    u = lax.broadcasted_iota(jnp.int32, (units, units), 0)
    v = lax.broadcasted_iota(jnp.int32, (units, units), 1)
    named = owner[...]
    mine = jnp.sum(jnp.where(u == v, jnp.broadcast_to(named, (units, units)), 0), axis=1, keepdims=True)
    same = jnp.where((mine == named) & (u < v), 1, 0)
    slot = named * capacity + jnp.sum(same, axis=0, keepdims=True)
    place = jnp.where(
        lax.broadcasted_iota(jnp.int32, (slots, units), 0) == slot, 1.0, 0.0
    ).astype(BF)
    for j in range(8):
        even = rows[pl.ds(2 * j, units, stride=16), :]
        odd = rows[pl.ds(2 * j + 1, units, stride=16), :]
        unit = (even + odd).astype(BF)
        sent = jnp.dot(place, unit, preferred_element_type=F32)
        out[:, :, j * C : (j + 1) * C] = sent.reshape(strips, capacity, C).astype(BF)


VM = pl.BlockSpec(memory_space=pltpu.VMEM)
HB = pl.BlockSpec(memory_space=pltpu.HBM)


def field(*lead, dtype=BF):
    return jax.ShapeDtypeStruct((*lead, COLS, C), dtype)


def run(kernel, outs, args, units, scratch=None, in_specs=None):
    if scratch is None:
        scratch = [pltpu.VMEM((4, 12, COLS, C), BF)]
    single = not isinstance(outs, list)
    moved = sum(a.size * a.dtype.itemsize for a in args)
    return pl.pallas_call(
        kernel,
        out_shape=outs,
        in_specs=in_specs or [VM] * len(args),
        out_specs=VM if single else [VM] * len(outs),
        scratch_shapes=scratch,
        compiler_params=pltpu.CompilerParams(vmem_limit_bytes=40 << 20),
        cost_estimate=pl.CostEstimate(
            flops=units * COLS * 27 * C * C * 2, bytes_accessed=moved, transcendentals=0
        ),
        name=kernel.__name__,
    )(*args)


def in_hbm(x):
    return pltpu.with_memory_space_constraint(x, pltpu.HBM)


def on_device(pixel_cot, frame_group, advantage, block_in, conv1_weight, conv2_weight, owner_map):
    times, strips = lax.axis_size("tm"), lax.axis_size("space")

    inner_pairs = [(s, s ^ 1) for s in range(strips)]
    outer_pairs = [(s, (s + 1 if s % 2 else s - 1) % strips) for s in range(strips)]
    later = [((t + 1) % times, t) for t in range(times)]
    sooner = [(t, (t + 1) % times) for t in range(times)]

    def swap_in(x):
        return lax.ppermute(x, "space", inner_pairs)

    def swap_out(x):
        return lax.ppermute(x, "space", outer_pairs)

    def from_later(x):
        return lax.ppermute(x, "tm", later)

    def corner(x, steps, pairs):
        route = [(a * strips + s, b * strips + r) for a, b in steps for s, r in pairs]
        return lax.ppermute(x, ("tm", "space"), route)

    def from_sooner(x):
        return lax.ppermute(x, "tm", sooner)

    w1, w2 = conv1_weight, conv2_weight
    bi = block_in
    ext = pltpu.VMEM((4, 12, COLS, C), BF)

    ten, eight = field(2, 10, dtype=F32), field(2, 8, dtype=F32)
    edges = [field(2, 8), field(6), field(6)]

    v0, rin, rout, b1x, dpi, dpo = run(
        start_kernel,
        [
            field(4, 8), field(3, 4, 2), field(3, 4, 2), field(2, 8), field(2, 2), field(2, 2),
        ],
        tuple(in_hbm(x) for x in (pixel_cot, bi, frame_group, advantage)),
        1,
        scratch=[
            pltpu.VMEM((4, 8, COLS, C), BF),
            pltpu.SMEM(frame_group.shape, jnp.int32),
            pltpu.SMEM(advantage.shape, F32),
            pltpu.SemaphoreType.DMA((13,)),
        ],
        in_specs=[HB] * 4,
    )
    b1x = from_sooner(b1x)
    rout, rin = swap_out(rout), swap_in(rin)
    dpo, dpi = corner(dpo, sooner, outer_pairs), corner(dpi, sooner, inner_pairs)
    v0x = from_later(run(extend_kernel, field(2, 10), (v0, rin, rout), 1, scratch=[]))
    taps = jax.ShapeDtypeStruct((1, *w1.shape[1:]), BF)
    bi1, w2late, w1late = run(
        fetch_kernel,
        [field(4, 8), taps, taps],
        (v0, in_hbm(bi), in_hbm(w2), in_hbm(w1)),
        1,
        scratch=[pltpu.SemaphoreType.DMA((3,))],
        in_specs=[VM, HB, HB, HB],
    )
    ga, ga23, d1, pre = run(
        early_kernel,
        [ten, eight, eight, ten],
        (v0, bi1, rin, rout, w2late, w1late),
        54,
        scratch=[ext, ext],
    )
    v1x = run(
        pre01_kernel,
        field(2, 10),
        (b1x, dpi, dpo, ga, pre, w1),
        10,
        scratch=[pltpu.VMEM((2, 12, COLS, C), BF)],
    )
    v1xr = from_later(v1x)
    v1, ein, eout = run(pre23_kernel, edges, (ga23, v0x, d1, v1x, w2), 8)
    r1out, r1in = swap_out(eout), swap_in(ein)
    b0x = run(extend0_kernel, field(2, 12), (bi, rin, rout, v1), 1, scratch=[])
    b0x = from_sooner(b0x)
    base01, base23 = run(
        inner_up_kernel,
        [ten, eight],
        (v1x, v1, v0, rin, rout, w1),
        28,
        scratch=[ext, pltpu.VMEM((2, 12, COLS, C), BF)],
    )
    v2x = run(up01_kernel, field(2, 10), (base01, r1in, r1out, w1), 8, scratch=[])
    v2xr = from_later(v2x)
    v2, ein, eout = run(up23_kernel, edges, (base23, r1in, r1out, v1xr, v2x, w1), 10)
    r2out, r2in = swap_out(eout), swap_in(ein)
    d0a = run(factor01_kernel, ten, (bi, rin, rout, b0x, v2, w1), 20)
    base01, base23 = run(inner_grad_kernel, [ten, eight], (v2x, v2, d0a, w2), 28)
    d0 = run(factor23_kernel, eight, (bi, rin, rout, base23, w1), 16)
    v3x = run(grad01_kernel, field(2, 10), (base01, r2in, r2out, d0a, d0, w2), 8, scratch=[])
    v3xr = from_later(v3x)
    v3, ein, eout = run(
        grad23_kernel,
        [field(2, 8), field(2), field(2)],
        (base23, r2in, r2out, v2xr, d0, w2),
        10,
    )
    r3out, r3in = swap_out(eout), swap_in(ein)
    base = run(inner_last_kernel, field(4, 8, dtype=F32), (v3x, v3, v2x, v2, w1), 24)
    owner = owner_map.reshape(1, -1)
    units = owner.shape[1]
    capacity = max(2, 2 * units // strips)
    outgoing = run(
        last_kernel,
        jax.ShapeDtypeStruct((strips, capacity, 8 * C), BF),
        (base, r3in, r3out, v3xr, owner, w1),
        8,
        scratch=[ext, pltpu.VMEM((4 * 4 * COLS, C), F32)],
    )
    arrived = lax.all_to_all(outgoing, "space", split_axis=0, concat_axis=0, tiled=True)
    return arrived.reshape(1, 1, strips, capacity, 8 * C)


def solution(mesh):
    in_specs = (
        P("tm", "space", None, None),
        P("tm"),
        P(),
        P(None, "tm", "space", None, None),
        P(),
        P(),
        P("tm", "space", None, None),
    )
    out_specs = P("tm", "space", None, None, None)
    return jax.shard_map(
        on_device, mesh=mesh, in_specs=in_specs, out_specs=out_specs, check_vma=False
    )
```

```python
import jax
import jax.numpy as jnp
from jax import lax
from jax.experimental import pallas as pl
from jax.experimental.pallas import tpu as pltpu
from jax.sharding import PartitionSpec as P

COLS = 64
C = 128
BF = jnp.bfloat16
F32 = jnp.float32


def side():
    return lax.rem(lax.axis_index("space"), 2)


def shift_add(partial):
    m = partial.shape[0]
    col = lax.broadcasted_iota(jnp.int32, (m, C), 0) % COLS
    low = jnp.where(col == 0, 0.0, pltpu.roll(partial[:, :C], 1, 0))
    high = jnp.where(col == COLS - 1, 0.0, pltpu.roll(partial[:, 2 * C :], m - 1, 0))
    return low + partial[:, C : 2 * C] + high


def patches(ext, t, r0, nr, steps=(0, 1, 2)):
    return jnp.concatenate(
        [
            ext[t + dt, r0 + dr : r0 + dr + nr].reshape(nr * COLS, C)
            for dt in steps
            for dr in range(3)
        ],
        axis=1,
    )


def back_taps(lhs, w, layer, steps=(0, 1, 2), rows=(0, 1, 2)):
    rhs = jnp.concatenate(
        [
            jnp.concatenate([w[layer, 2 - dt, 2 - dr, 2 - j] for j in range(3)], axis=0)
            for dt in steps
            for dr in rows
        ],
        axis=1,
    )
    return shift_add(
        lax.dot_general(lhs, rhs, (((1,), (1,)), ((), ())), preferred_element_type=F32)
    )


def conv_back(ext, w, layer, t, r0, nr, steps=(0, 1, 2)):
    return back_taps(patches(ext, t, r0, nr, steps), w, layer, steps).reshape(nr, COLS, C)


def conv_fore(ext, w, layer, t, r0, nr, steps=(0, 1, 2)):
    rhs = jnp.concatenate(
        [
            jnp.concatenate([w[layer, dt, dr, j] for j in range(3)], axis=1)
            for dt in steps
            for dr in range(3)
        ],
        axis=0,
    )
    out = jnp.dot(patches(ext, t, r0, nr, steps), rhs, preferred_element_type=F32)
    return shift_add(out).reshape(nr, COLS, C)


def factor(pre):
    s = jax.nn.sigmoid(pre)
    return s * (1.0 + pre * (1.0 - s))


def inside(outer):
    s = lax.axis_index("space")
    end = (s == 0) | (s == lax.axis_size("space") - 1)
    return jnp.where(end, jnp.zeros_like(outer), outer)


def with_later(halo):
    last = lax.axis_index("tm") == lax.axis_size("tm") - 1
    return jnp.where(last, jnp.zeros_like(halo), halo)


def with_sooner(halo):
    return jnp.where(lax.axis_index("tm") == 0, jnp.zeros_like(halo), halo)


def put_edges(ext, frames, inner, outer):
    p = side()
    ext[frames, pl.ds(10 * (1 - p), 2)] = inner
    ext[frames, pl.ds(10 * p, 2)] = inside(outer)


def store_ten(out, t, value):
    value = value.astype(BF)
    s = lax.axis_index("space")
    zero = jnp.zeros((1, COLS, C), BF)
    out[t, 1:9] = value[1:9]
    out[t, 0:1] = jnp.where(s == 0, zero, value[0:1])
    out[t, 9:10] = jnp.where(s == lax.axis_size("space") - 1, zero, value[9:10])


def send_edges(first, late, ein, eout):
    p = side()
    for t in range(2):
        ein[t], eout[t] = first[t, 7 - 5 * p], first[t, 2 + 5 * p]
        for k in range(2):
            ein[2 + 2 * t + k] = late[t, 6 * (1 - p) + k]
            eout[2 + 2 * t + k] = late[t, 6 * p + k]


def start_kernel(
    cot, bi, group, adv, v0, rin, rout, b1s, dpi, dpo, raw, gs, ads, sem
):
    p = side()
    inner, outer = pl.ds(6 * (1 - p), 2), pl.ds(6 * p, 2)
    copies = [
        pltpu.make_async_copy(group, gs, sem.at[0]),
        pltpu.make_async_copy(adv, ads, sem.at[1]),
    ]
    copies += [pltpu.make_async_copy(cot.at[t], raw.at[t], sem.at[2 + t]) for t in range(4)]
    copies += [
        pltpu.make_async_copy(bi.at[1, pl.ds(2, 2)], b1s, sem.at[6]),
        pltpu.make_async_copy(bi.at[1, :, inner], rin.at[1], sem.at[7]),
        pltpu.make_async_copy(bi.at[1, :, outer], rout.at[1], sem.at[8]),
        pltpu.make_async_copy(bi.at[1, pl.ds(2, 2), inner], dpi, sem.at[9]),
        pltpu.make_async_copy(bi.at[1, pl.ds(2, 2), outer], dpo, sem.at[10]),
        pltpu.make_async_copy(bi.at[0, :, inner], rin.at[2], sem.at[11]),
        pltpu.make_async_copy(bi.at[0, :, outer], rout.at[2], sem.at[12]),
    ]
    for copy in copies:
        copy.start()
    copies[0].wait()
    copies[1].wait()
    for t in range(4):
        copies[2 + t].wait()
        scale = ads[gs[t]]
        v0[t] = (raw[t].astype(F32) * scale).astype(BF)
        rin[0, t] = (raw[t, inner].astype(F32) * scale).astype(BF)
        rout[0, t] = (raw[t, outer].astype(F32) * scale).astype(BF)
    for copy in copies[6:]:
        copy.wait()


def extend_kernel(v0, rin, rout, vx):
    p = side()
    for t in range(2):
        vx[t, 1:9] = v0[t]
        vx[t, 9 * (1 - p)] = rin[0, t, p]
        vx[t, 9 * p] = inside(rout[0, t, 1 - p])


def extend0_kernel(bi, rin, rout, after, bx):
    bx[:, 2:10] = bi[0, 2:4]
    put_edges(bx, slice(0, 2), rin[2, 2:4], rout[2, 2:4])


def fetch_kernel(after, bi, w2, w1, bi1, w2o, w1o, sem):
    copies = [
        pltpu.make_async_copy(w2.at[pl.ds(1, 1)], w2o, sem.at[0]),
        pltpu.make_async_copy(w1.at[pl.ds(1, 1)], w1o, sem.at[1]),
        pltpu.make_async_copy(bi.at[1], bi1, sem.at[2]),
    ]
    for copy in copies:
        copy.start()
    for copy in copies:
        copy.wait()


def early_kernel(v0, bi1, rin, rout, w2, w1, ga, ga23, d1, pre, ext, ext1):
    ext[:, 2:10] = v0[...]
    put_edges(ext, slice(0, 4), rin[0], rout[0])
    for t in range(2):
        ga[t] = conv_back(ext, w2, 0, t, 0, 10)
    for t, steps in ((0, (0, 1)), (1, (0,))):
        ga23[t] = conv_back(ext, w2, 0, 2 + t, 1, 8, steps)
    ext1[:, 2:10] = bi1[...]
    put_edges(ext1, slice(0, 4), rin[1], rout[1])
    for t in range(2):
        d1[t] = factor(conv_fore(ext1, w1, 0, t, 1, 8))
    for t, steps in ((0, (2,)), (1, (1, 2))):
        pre[t] = conv_fore(ext1, w1, 0, t - 2, 0, 10, steps)


def pre01_kernel(bx, dpi, dpo, ga, pre, w1, v1x, ext):
    ext[:, 2:10] = with_sooner(bx[...])
    put_edges(ext, slice(0, 2), with_sooner(dpi[...]), with_sooner(dpo[...]))
    for t, steps in ((0, (0, 1)), (1, (0,))):
        whole = pre[t] + conv_fore(ext, w1, 1, t, 0, 10, steps)
        store_ten(v1x, t, ga[t] * factor(whole))


def factor01_kernel(bi, rin, rout, bx, after, w1, d, ext):
    ext[0:2] = with_sooner(bx[...])
    ext[2:4, 2:10] = bi[0, 0:2]
    put_edges(ext, slice(2, 4), rin[2, 0:2], rout[2, 0:2])
    for t in range(2):
        d[t] = factor(conv_fore(ext, w1, 0, t, 0, 10))


def factor23_kernel(bi, rin, rout, after, w1, d, ext):
    ext[:, 2:10] = bi[0]
    put_edges(ext, slice(0, 4), rin[2], rout[2])
    for t in range(2):
        d[t] = factor(conv_fore(ext, w1, 0, t, 1, 8))


def later_part(ext, w, layer):
    return [
        conv_back(ext, w, layer, t, 1, 8, steps) for t, steps in ((0, (2,)), (1, (1, 2)))
    ]


def pre23_kernel(ga23, vx, d, v1x, w2, v1, ein, eout, ext):
    ext[2:4, 1:11] = with_later(vx[...])
    for t, more in enumerate(later_part(ext, w2, 1)):
        v1[t] = ((ga23[t] + more) * d[t]).astype(BF)
    send_edges(v1x, v1, ein, eout)


def up01_kernel(base01, rin, rout, after, w1, v2x):
    top, bottom = rim_rows(*halos(rin, rout), w1, 1)
    for t in range(2):
        store_ten(v2x, t, ten_rows(base01, t, top, bottom))


def grad01_kernel(base01, rin, rout, d, w2, v3x):
    top, bottom = rim_rows(*halos(rin, rout), w2, 0)
    for t in range(2):
        store_ten(v3x, t, ten_rows(base01, t, top, bottom) * d[t])


def whole23(base23, rin, rout, vxr, w, layer, ext):
    ext[2:4, 1:11] = with_later(vxr[...])
    above, below = halos(rin, rout)
    top = edge_rows([above[3], above[5]], w, layer, 0, 2)
    bottom = edge_rows([below[2], below[4]], w, layer, 2, 2)
    more = later_part(ext, w, layer)
    return [eight_rows(base23, t, top, bottom) + more[t] for t in range(2)]


def up23_kernel(base23, rin, rout, vxr, v2x, w1, v2, ein, eout, ext):
    for t, whole in enumerate(whole23(base23, rin, rout, vxr, w1, 1, ext)):
        v2[t] = whole.astype(BF)
    send_edges(v2x, v2, ein, eout)


def grad23_kernel(base23, rin, rout, vxr, d, w2, v3, ein, eout, ext):
    for t, whole in enumerate(whole23(base23, rin, rout, vxr, w2, 0, ext)):
        v3[t] = (whole * d[t]).astype(BF)
    p = side()
    for t in range(2):
        ein[t], eout[t] = v3[t, 7 * (1 - p)], v3[t, 7 * p]


def row_pairs(up):
    up = up.astype(BF).astype(F32).reshape(4, 2, COLS, C)
    return up[:, 0] + up[:, 1]


def inner_last_kernel(v3x, v3, v2x, v2, w1, base, ext):
    ext[0:2, 1:11] = v3x[...]
    ext[2:4, 2:10] = v3[...]
    ext[2:4, 1:2] = jnp.zeros((2, 1, COLS, C), BF)
    ext[2:4, 10:11] = jnp.zeros((2, 1, COLS, C), BF)
    for t in range(2):
        base[t] = v2x[t, 1:9].astype(F32) + conv_back(ext, w1, 0, t, 1, 8)
    for t, steps in ((0, (0, 1)), (1, (0,))):
        base[2 + t] = v2[t].astype(F32) + conv_back(ext, w1, 0, 2 + t, 1, 8, steps)


def edge_rows(halo, w, layer, dr, first=0):
    zero = jnp.zeros((COLS, C), BF)
    frames = [zero, zero, halo[0], halo[1], zero, zero]
    lhs = [jnp.concatenate(frames[t : t + 3], axis=1) for t in range(first, 4)]
    out = back_taps(jnp.concatenate(lhs, axis=0), w, layer, rows=(dr,))
    return out.reshape(4 - first, 1, COLS, C)


def halos(rin, rout):
    low, near, far = side() == 1, rin[...], inside(rout[...])
    return jnp.where(low, near, far), jnp.where(low, far, near)


def rim_rows(above, below, w, layer):
    zero = jnp.zeros((COLS, C), BF)
    up = [(above[0], zero), (above[1], zero), (above[2], above[3]), (above[4], above[5])]
    down = [(zero, below[0]), (zero, below[1]), (below[2], below[3]), (below[4], below[5])]
    tops, bottoms = [], []
    for t in range(2):
        three = range(t, t + 3)
        tops += [
            [x for f in three for x in up[f]],
            [x for f in three for x in (up[f][1], zero)],
        ]
        bottoms += [
            [x for f in three for x in (zero, down[f][0])],
            [x for f in three for x in down[f]],
        ]
    out = []
    for lines, rows in ((tops, (0, 1)), (bottoms, (1, 2))):
        lhs = jnp.concatenate([jnp.concatenate(line, axis=1) for line in lines], axis=0)
        out.append(back_taps(lhs, w, layer, rows=rows).reshape(2, 2, COLS, C))
    return out


def local_part(ext, vx, v, w, layer):
    ext[0:2, 1:11] = vx[...]
    ext[2:4, 2:10] = v[...]
    for frames, edge in ((slice(0, 2), 1), (slice(2, 4), 2)):
        ext[frames, 0:edge] = jnp.zeros((2, edge, COLS, C), BF)
        ext[frames, 12 - edge : 12] = jnp.zeros((2, edge, COLS, C), BF)
    first = [conv_back(ext, w, layer, t, 0, 10) for t in range(2)]
    late = [
        conv_back(ext, w, layer, 2 + t, 1, 8, steps) for t, steps in ((0, (0, 1)), (1, (0,)))
    ]
    return first, late


def inner_up_kernel(v1x, v1, v0, r0in, r0out, w1, base01, base23, ext, old):
    old[:, 2:10] = v0[0:2]
    put_edges(old, slice(0, 2), r0in[0, 0:2], r0out[0, 0:2])
    first, late = local_part(ext, v1x, v1, w1, 1)
    for t in range(2):
        base01[t] = old[t, 1:11].astype(F32) + first[t]
        base23[t] = v0[2 + t].astype(F32) + late[t]


def inner_grad_kernel(v2x, v2, after, w2, base01, base23, ext):
    first, late = local_part(ext, v2x, v2, w2, 0)
    for t in range(2):
        base01[t], base23[t] = first[t], late[t]


def ten_rows(base, t, top, bottom):
    return jnp.concatenate(
        [base[t, 0:2] + top[t], base[t, 2:8], base[t, 8:10] + bottom[t]], axis=0
    )


def eight_rows(base, t, top, bottom):
    return jnp.concatenate(
        [base[t, 0:1] + top[t], base[t, 1:7], base[t, 7:8] + bottom[t]], axis=0
    )


def last_kernel(base, rin, rout, vxr, owner, w1, out, ext, rows):
    ext[2:4, 1:11] = with_later(vxr[...])
    above, below = halos(rin, rout)
    top, bottom = edge_rows(above, w1, 0, 0), edge_rows(below, w1, 0, 2)
    more = [0.0, 0.0, *later_part(ext, w1, 0)]
    for t in range(4):
        pair = row_pairs(eight_rows(base, t, top, bottom) + more[t])
        rows[t * 4 * COLS : (t + 1) * 4 * COLS] = pair.reshape(4 * COLS, C)
    units = owner.shape[1]
    strips, capacity = out.shape[0], out.shape[1]
    slots = strips * capacity
    u = lax.broadcasted_iota(jnp.int32, (units, units), 0)
    v = lax.broadcasted_iota(jnp.int32, (units, units), 1)
    named = owner[...]
    mine = jnp.sum(jnp.where(u == v, jnp.broadcast_to(named, (units, units)), 0), axis=1, keepdims=True)
    same = jnp.where((mine == named) & (u < v), 1, 0)
    slot = named * capacity + jnp.sum(same, axis=0, keepdims=True)
    place = jnp.where(
        lax.broadcasted_iota(jnp.int32, (slots, units), 0) == slot, 1.0, 0.0
    ).astype(BF)
    for j in range(8):
        even = rows[pl.ds(2 * j, units, stride=16), :]
        odd = rows[pl.ds(2 * j + 1, units, stride=16), :]
        unit = (even + odd).astype(BF)
        sent = jnp.dot(place, unit, preferred_element_type=F32)
        out[:, :, j * C : (j + 1) * C] = sent.reshape(strips, capacity, C).astype(BF)


VM = pl.BlockSpec(memory_space=pltpu.VMEM)
HB = pl.BlockSpec(memory_space=pltpu.HBM)


def field(*lead, dtype=BF):
    return jax.ShapeDtypeStruct((*lead, COLS, C), dtype)


def run(kernel, outs, args, units, scratch=None, in_specs=None):
    if scratch is None:
        scratch = [pltpu.VMEM((4, 12, COLS, C), BF)]
    single = not isinstance(outs, list)
    moved = sum(a.size * a.dtype.itemsize for a in args)
    return pl.pallas_call(
        kernel,
        out_shape=outs,
        in_specs=in_specs or [VM] * len(args),
        out_specs=VM if single else [VM] * len(outs),
        scratch_shapes=scratch,
        compiler_params=pltpu.CompilerParams(vmem_limit_bytes=40 << 20),
        cost_estimate=pl.CostEstimate(
            flops=units * COLS * 27 * C * C * 2, bytes_accessed=moved, transcendentals=0
        ),
        name=kernel.__name__,
    )(*args)


def in_hbm(x):
    return pltpu.with_memory_space_constraint(x, pltpu.HBM)


def on_device(pixel_cot, frame_group, advantage, block_in, conv1_weight, conv2_weight, owner_map):
    times, strips = lax.axis_size("tm"), lax.axis_size("space")

    inner_pairs = [(s, s ^ 1) for s in range(strips)]
    outer_pairs = [(s, (s + 1 if s % 2 else s - 1) % strips) for s in range(strips)]
    later = [((t + 1) % times, t) for t in range(times)]
    sooner = [(t, (t + 1) % times) for t in range(times)]

    def swap_in(x):
        return lax.ppermute(x, "space", inner_pairs)

    def swap_out(x):
        return lax.ppermute(x, "space", outer_pairs)

    def from_later(x):
        return lax.ppermute(x, "tm", later)

    def corner(x, steps, pairs):
        route = [(a * strips + s, b * strips + r) for a, b in steps for s, r in pairs]
        return lax.ppermute(x, ("tm", "space"), route)

    def from_sooner(x):
        return lax.ppermute(x, "tm", sooner)

    w1, w2 = conv1_weight, conv2_weight
    bi = block_in
    ext = pltpu.VMEM((4, 12, COLS, C), BF)

    ten, eight = field(2, 10, dtype=F32), field(2, 8, dtype=F32)
    edges = [field(2, 8), field(6), field(6)]

    v0, rin, rout, b1x, dpi, dpo = run(
        start_kernel,
        [
            field(4, 8), field(3, 4, 2), field(3, 4, 2), field(2, 8), field(2, 2), field(2, 2),
        ],
        tuple(in_hbm(x) for x in (pixel_cot, bi, frame_group, advantage)),
        1,
        scratch=[
            pltpu.VMEM((4, 8, COLS, C), BF),
            pltpu.SMEM(frame_group.shape, jnp.int32),
            pltpu.SMEM(advantage.shape, F32),
            pltpu.SemaphoreType.DMA((13,)),
        ],
        in_specs=[HB] * 4,
    )
    b1x = from_sooner(b1x)
    rout, rin = swap_out(rout), swap_in(rin)
    dpo, dpi = corner(dpo, sooner, outer_pairs), corner(dpi, sooner, inner_pairs)
    v0x = from_later(run(extend_kernel, field(2, 10), (v0, rin, rout), 1, scratch=[]))
    taps = jax.ShapeDtypeStruct((1, *w1.shape[1:]), BF)
    bi1, w2late, w1late = run(
        fetch_kernel,
        [field(4, 8), taps, taps],
        (v0, in_hbm(bi), in_hbm(w2), in_hbm(w1)),
        1,
        scratch=[pltpu.SemaphoreType.DMA((3,))],
        in_specs=[VM, HB, HB, HB],
    )
    ga, ga23, d1, pre = run(
        early_kernel,
        [ten, eight, eight, ten],
        (v0, bi1, rin, rout, w2late, w1late),
        54,
        scratch=[ext, ext],
    )
    v1x = run(
        pre01_kernel,
        field(2, 10),
        (b1x, dpi, dpo, ga, pre, w1),
        10,
        scratch=[pltpu.VMEM((2, 12, COLS, C), BF)],
    )
    v1xr = from_later(v1x)
    v1, ein, eout = run(pre23_kernel, edges, (ga23, v0x, d1, v1x, w2), 8)
    r1out, r1in = swap_out(eout), swap_in(ein)
    b0x = run(extend0_kernel, field(2, 12), (bi, rin, rout, v1), 1, scratch=[])
    b0x = from_sooner(b0x)
    base01, base23 = run(
        inner_up_kernel,
        [ten, eight],
        (v1x, v1, v0, rin, rout, w1),
        28,
        scratch=[ext, pltpu.VMEM((2, 12, COLS, C), BF)],
    )
    d0 = run(factor23_kernel, eight, (bi, rin, rout, base23, w1), 16)
    v2x = run(up01_kernel, field(2, 10), (base01, r1in, r1out, d0, w1), 8, scratch=[])
    v2xr = from_later(v2x)
    v2, ein, eout = run(up23_kernel, edges, (base23, r1in, r1out, v1xr, v2x, w1), 10)
    r2out, r2in = swap_out(eout), swap_in(ein)
    d0a = run(factor01_kernel, ten, (bi, rin, rout, b0x, v2, w1), 20)
    base01, base23 = run(inner_grad_kernel, [ten, eight], (v2x, v2, d0a, w2), 28)
    v3x = run(grad01_kernel, field(2, 10), (base01, r2in, r2out, d0a, w2), 8, scratch=[])
    v3xr = from_later(v3x)
    v3, ein, eout = run(
        grad23_kernel,
        [field(2, 8), field(2), field(2)],
        (base23, r2in, r2out, v2xr, d0, w2),
        10,
    )
    r3out, r3in = swap_out(eout), swap_in(ein)
    base = run(inner_last_kernel, field(4, 8, dtype=F32), (v3x, v3, v2x, v2, w1), 24)
    owner = owner_map.reshape(1, -1)
    units = owner.shape[1]
    capacity = max(2, 2 * units // strips)
    outgoing = run(
        last_kernel,
        jax.ShapeDtypeStruct((strips, capacity, 8 * C), BF),
        (base, r3in, r3out, v3xr, owner, w1),
        8,
        scratch=[ext, pltpu.VMEM((4 * 4 * COLS, C), F32)],
    )
    arrived = lax.all_to_all(outgoing, "space", split_axis=0, concat_axis=0, tiled=True)
    return arrived.reshape(1, 1, strips, capacity, 8 * C)


def solution(mesh):
    in_specs = (
        P("tm", "space", None, None),
        P("tm"),
        P(),
        P(None, "tm", "space", None, None),
        P(),
        P(),
        P("tm", "space", None, None),
    )
    out_specs = P("tm", "space", None, None, None)
    return jax.shard_map(
        on_device, mesh=mesh, in_specs=in_specs, out_specs=out_specs, check_vma=False
    )
```

```python
import jax
import jax.numpy as jnp
from jax import lax
from jax.experimental import pallas as pl
from jax.experimental.pallas import tpu as pltpu
from jax.sharding import PartitionSpec as P

COLS = 64
C = 128
BF = jnp.bfloat16
F32 = jnp.float32


def side():
    return lax.rem(lax.axis_index("space"), 2)


def shift_add(partial):
    m = partial.shape[0]
    col = lax.broadcasted_iota(jnp.int32, (m, C), 0) % COLS
    low = jnp.where(col == 0, 0.0, pltpu.roll(partial[:, :C], 1, 0))
    high = jnp.where(col == COLS - 1, 0.0, pltpu.roll(partial[:, 2 * C :], m - 1, 0))
    return low + partial[:, C : 2 * C] + high


def patches(ext, t, r0, nr, steps=(0, 1, 2)):
    return jnp.concatenate(
        [
            ext[t + dt, r0 + dr : r0 + dr + nr].reshape(nr * COLS, C)
            for dt in steps
            for dr in range(3)
        ],
        axis=1,
    )


def back_taps(lhs, w, layer, steps=(0, 1, 2), rows=(0, 1, 2)):
    rhs = jnp.concatenate(
        [
            jnp.concatenate([w[layer, 2 - dt, 2 - dr, 2 - j] for j in range(3)], axis=0)
            for dt in steps
            for dr in rows
        ],
        axis=1,
    )
    return shift_add(
        lax.dot_general(lhs, rhs, (((1,), (1,)), ((), ())), preferred_element_type=F32)
    )


def conv_back(ext, w, layer, t, r0, nr, steps=(0, 1, 2)):
    return back_taps(patches(ext, t, r0, nr, steps), w, layer, steps).reshape(nr, COLS, C)


def conv_fore(ext, w, layer, t, r0, nr, steps=(0, 1, 2)):
    rhs = jnp.concatenate(
        [
            jnp.concatenate([w[layer, dt, dr, j] for j in range(3)], axis=1)
            for dt in steps
            for dr in range(3)
        ],
        axis=0,
    )
    out = jnp.dot(patches(ext, t, r0, nr, steps), rhs, preferred_element_type=F32)
    return shift_add(out).reshape(nr, COLS, C)


def factor(pre):
    s = jax.nn.sigmoid(pre)
    return s * (1.0 + pre * (1.0 - s))


def inside(outer):
    s = lax.axis_index("space")
    end = (s == 0) | (s == lax.axis_size("space") - 1)
    return jnp.where(end, jnp.zeros_like(outer), outer)


def with_later(halo):
    last = lax.axis_index("tm") == lax.axis_size("tm") - 1
    return jnp.where(last, jnp.zeros_like(halo), halo)


def with_sooner(halo):
    return jnp.where(lax.axis_index("tm") == 0, jnp.zeros_like(halo), halo)


def put_edges(ext, frames, inner, outer):
    p = side()
    ext[frames, pl.ds(10 * (1 - p), 2)] = inner
    ext[frames, pl.ds(10 * p, 2)] = inside(outer)


def store_ten(out, t, value):
    value = value.astype(BF)
    s = lax.axis_index("space")
    zero = jnp.zeros((1, COLS, C), BF)
    out[t, 1:9] = value[1:9]
    out[t, 0:1] = jnp.where(s == 0, zero, value[0:1])
    out[t, 9:10] = jnp.where(s == lax.axis_size("space") - 1, zero, value[9:10])


def send_edges(first, late, ein, eout):
    p = side()
    for t in range(2):
        ein[t], eout[t] = first[t, 7 - 5 * p], first[t, 2 + 5 * p]
        for k in range(2):
            ein[2 + 2 * t + k] = late[t, 6 * (1 - p) + k]
            eout[2 + 2 * t + k] = late[t, 6 * p + k]


def start_kernel(
    cot, bi, group, adv, v0, rin, rout, b1s, dpi, dpo, raw, gs, ads, sem
):
    p = side()
    inner, outer = pl.ds(6 * (1 - p), 2), pl.ds(6 * p, 2)
    copies = [
        pltpu.make_async_copy(group, gs, sem.at[0]),
        pltpu.make_async_copy(adv, ads, sem.at[1]),
    ]
    copies += [pltpu.make_async_copy(cot.at[t], raw.at[t], sem.at[2 + t]) for t in range(4)]
    copies += [
        pltpu.make_async_copy(bi.at[1, pl.ds(2, 2)], b1s, sem.at[6]),
        pltpu.make_async_copy(bi.at[1, :, inner], rin.at[1], sem.at[7]),
        pltpu.make_async_copy(bi.at[1, :, outer], rout.at[1], sem.at[8]),
        pltpu.make_async_copy(bi.at[1, pl.ds(2, 2), inner], dpi, sem.at[9]),
        pltpu.make_async_copy(bi.at[1, pl.ds(2, 2), outer], dpo, sem.at[10]),
        pltpu.make_async_copy(bi.at[0, :, inner], rin.at[2], sem.at[11]),
        pltpu.make_async_copy(bi.at[0, :, outer], rout.at[2], sem.at[12]),
    ]
    for copy in copies:
        copy.start()
    copies[0].wait()
    copies[1].wait()
    for t in range(4):
        copies[2 + t].wait()
        scale = ads[gs[t]]
        v0[t] = (raw[t].astype(F32) * scale).astype(BF)
        rin[0, t] = (raw[t, inner].astype(F32) * scale).astype(BF)
        rout[0, t] = (raw[t, outer].astype(F32) * scale).astype(BF)
    for copy in copies[6:]:
        copy.wait()


def extend_kernel(v0, rin, rout, vx):
    p = side()
    for t in range(2):
        vx[t, 1:9] = v0[t]
        vx[t, 9 * (1 - p)] = rin[0, t, p]
        vx[t, 9 * p] = inside(rout[0, t, 1 - p])


def extend0_kernel(bi, rin, rout, after, bx):
    bx[:, 2:10] = bi[0, 2:4]
    put_edges(bx, slice(0, 2), rin[2, 2:4], rout[2, 2:4])


def fetch_kernel(after, bi, w2, w1, bi1, w2o, w1o, sem):
    copies = [
        pltpu.make_async_copy(w2.at[pl.ds(1, 1)], w2o, sem.at[0]),
        pltpu.make_async_copy(w1.at[pl.ds(1, 1)], w1o, sem.at[1]),
        pltpu.make_async_copy(bi.at[1], bi1, sem.at[2]),
    ]
    for copy in copies:
        copy.start()
    for copy in copies:
        copy.wait()


def early_kernel(v0, bi1, rin, rout, w2, w1, ga, ga23, d1, pre, ext, ext1):
    ext[:, 2:10] = v0[...]
    put_edges(ext, slice(0, 4), rin[0], rout[0])
    for t in range(2):
        ga[t] = conv_back(ext, w2, 0, t, 0, 10)
    for t, steps in ((0, (0, 1)), (1, (0,))):
        ga23[t] = conv_back(ext, w2, 0, 2 + t, 1, 8, steps)
    ext1[:, 2:10] = bi1[...]
    put_edges(ext1, slice(0, 4), rin[1], rout[1])
    for t in range(2):
        d1[t] = factor(conv_fore(ext1, w1, 0, t, 1, 8))
    for t, steps in ((0, (2,)), (1, (1, 2))):
        pre[t] = conv_fore(ext1, w1, 0, t - 2, 0, 10, steps)


def pre01_kernel(bx, dpi, dpo, ga, pre, w1, v1x, ext):
    ext[:, 2:10] = with_sooner(bx[...])
    put_edges(ext, slice(0, 2), with_sooner(dpi[...]), with_sooner(dpo[...]))
    for t, steps in ((0, (0, 1)), (1, (0,))):
        whole = pre[t] + conv_fore(ext, w1, 1, t, 0, 10, steps)
        store_ten(v1x, t, ga[t] * factor(whole))


def factor01_kernel(bi, rin, rout, bx, after, w1, d, ext):
    ext[0:2] = with_sooner(bx[...])
    ext[2:4, 2:10] = bi[0, 0:2]
    put_edges(ext, slice(2, 4), rin[2, 0:2], rout[2, 0:2])
    for t in range(2):
        d[t] = factor(conv_fore(ext, w1, 0, t, 0, 10))


def factor23_kernel(bi, rin, rout, after, w1, d, ext):
    ext[:, 2:10] = bi[0]
    put_edges(ext, slice(0, 4), rin[2], rout[2])
    for t in range(2):
        d[t] = factor(conv_fore(ext, w1, 0, t, 1, 8))


def later_part(ext, w, layer):
    return [
        conv_back(ext, w, layer, t, 1, 8, steps) for t, steps in ((0, (2,)), (1, (1, 2)))
    ]


def pre23_kernel(ga23, vx, d, v1x, w2, v1, ein, eout, ext):
    ext[2:4, 1:11] = with_later(vx[...])
    for t, more in enumerate(later_part(ext, w2, 1)):
        v1[t] = ((ga23[t] + more) * d[t]).astype(BF)
    send_edges(v1x, v1, ein, eout)


def up01_kernel(base01, rin, rout, after, w1, v2x):
    top, bottom = rim_rows(*halos(rin, rout), w1, 1)
    for t in range(2):
        store_ten(v2x, t, ten_rows(base01, t, top, bottom))


def grad01_kernel(base01, rin, rout, d, w2, v3x):
    top, bottom = rim_rows(*halos(rin, rout), w2, 0)
    for t in range(2):
        store_ten(v3x, t, ten_rows(base01, t, top, bottom) * d[t])


def whole23(base23, rin, rout, vxr, w, layer, ext):
    ext[2:4, 1:11] = with_later(vxr[...])
    above, below = halos(rin, rout)
    top = edge_rows([above[3], above[5]], w, layer, 0, 2)
    bottom = edge_rows([below[2], below[4]], w, layer, 2, 2)
    more = later_part(ext, w, layer)
    return [eight_rows(base23, t, top, bottom) + more[t] for t in range(2)]


def up23_kernel(base23, rin, rout, vxr, v2x, w1, v2, ein, eout, ext):
    for t, whole in enumerate(whole23(base23, rin, rout, vxr, w1, 1, ext)):
        v2[t] = whole.astype(BF)
    send_edges(v2x, v2, ein, eout)


def grad23_kernel(base23, rin, rout, vxr, d, w2, v3, ein, eout, ext):
    for t, whole in enumerate(whole23(base23, rin, rout, vxr, w2, 0, ext)):
        v3[t] = (whole * d[t]).astype(BF)
    p = side()
    for t in range(2):
        ein[t], eout[t] = v3[t, 7 * (1 - p)], v3[t, 7 * p]


def row_pairs(up):
    up = up.astype(BF).astype(F32).reshape(4, 2, COLS, C)
    return up[:, 0] + up[:, 1]


def inner_last_kernel(v3x, v3, v2x, v2, w1, base, ext):
    ext[0:2, 1:11] = v3x[...]
    ext[2:4, 2:10] = v3[...]
    ext[2:4, 1:2] = jnp.zeros((2, 1, COLS, C), BF)
    ext[2:4, 10:11] = jnp.zeros((2, 1, COLS, C), BF)
    for t in range(2):
        base[t] = v2x[t, 1:9].astype(F32) + conv_back(ext, w1, 0, t, 1, 8)
    for t, steps in ((0, (0, 1)), (1, (0,))):
        base[2 + t] = v2[t].astype(F32) + conv_back(ext, w1, 0, 2 + t, 1, 8, steps)


def edge_rows(halo, w, layer, dr, first=0):
    zero = jnp.zeros((COLS, C), BF)
    frames = [zero, zero, halo[0], halo[1], zero, zero]
    lhs = [jnp.concatenate(frames[t : t + 3], axis=1) for t in range(first, 4)]
    out = back_taps(jnp.concatenate(lhs, axis=0), w, layer, rows=(dr,))
    return out.reshape(4 - first, 1, COLS, C)


def halos(rin, rout):
    low, near, far = side() == 1, rin[...], inside(rout[...])
    return jnp.where(low, near, far), jnp.where(low, far, near)


def rim_rows(above, below, w, layer):
    zero = jnp.zeros((COLS, C), BF)
    up = [(above[0], zero), (above[1], zero), (above[2], above[3]), (above[4], above[5])]
    down = [(zero, below[0]), (zero, below[1]), (below[2], below[3]), (below[4], below[5])]
    tops, bottoms = [], []
    for t in range(2):
        three = range(t, t + 3)
        tops += [
            [x for f in three for x in up[f]],
            [x for f in three for x in (up[f][1], zero)],
        ]
        bottoms += [
            [x for f in three for x in (zero, down[f][0])],
            [x for f in three for x in down[f]],
        ]
    out = []
    for lines, rows in ((tops, (0, 1)), (bottoms, (1, 2))):
        lhs = jnp.concatenate([jnp.concatenate(line, axis=1) for line in lines], axis=0)
        out.append(back_taps(lhs, w, layer, rows=rows).reshape(2, 2, COLS, C))
    return out


def local_part(ext, vx, v, w, layer):
    ext[0:2, 1:11] = vx[...]
    ext[2:4, 2:10] = v[...]
    for frames, edge in ((slice(0, 2), 1), (slice(2, 4), 2)):
        ext[frames, 0:edge] = jnp.zeros((2, edge, COLS, C), BF)
        ext[frames, 12 - edge : 12] = jnp.zeros((2, edge, COLS, C), BF)
    first = [conv_back(ext, w, layer, t, 0, 10) for t in range(2)]
    late = [
        conv_back(ext, w, layer, 2 + t, 1, 8, steps) for t, steps in ((0, (0, 1)), (1, (0,)))
    ]
    return first, late


def inner_up_kernel(v1x, v1, v0, r0in, r0out, w1, base01, base23, ext, old):
    old[:, 2:10] = v0[0:2]
    put_edges(old, slice(0, 2), r0in[0, 0:2], r0out[0, 0:2])
    first, late = local_part(ext, v1x, v1, w1, 1)
    for t in range(2):
        base01[t] = old[t, 1:11].astype(F32) + first[t]
        base23[t] = v0[2 + t].astype(F32) + late[t]


def inner_grad_kernel(v2x, v2, after, w2, base01, base23, ext):
    first, late = local_part(ext, v2x, v2, w2, 0)
    for t in range(2):
        base01[t], base23[t] = first[t], late[t]


def ten_rows(base, t, top, bottom):
    return jnp.concatenate(
        [base[t, 0:2] + top[t], base[t, 2:8], base[t, 8:10] + bottom[t]], axis=0
    )


def eight_rows(base, t, top, bottom):
    return jnp.concatenate(
        [base[t, 0:1] + top[t], base[t, 1:7], base[t, 7:8] + bottom[t]], axis=0
    )


def last_kernel(base, rin, rout, vxr, owner, w1, out, ext, rows):
    ext[2:4, 1:11] = with_later(vxr[...])
    above, below = halos(rin, rout)
    top, bottom = edge_rows(above, w1, 0, 0), edge_rows(below, w1, 0, 2)
    more = [0.0, 0.0, *later_part(ext, w1, 0)]
    for t in range(4):
        pair = row_pairs(eight_rows(base, t, top, bottom) + more[t])
        rows[t * 4 * COLS : (t + 1) * 4 * COLS] = pair.reshape(4 * COLS, C)
    units = owner.shape[1]
    strips, capacity = out.shape[0], out.shape[1]
    slots = strips * capacity
    u = lax.broadcasted_iota(jnp.int32, (units, units), 0)
    v = lax.broadcasted_iota(jnp.int32, (units, units), 1)
    named = owner[...]
    mine = jnp.sum(jnp.where(u == v, jnp.broadcast_to(named, (units, units)), 0), axis=1, keepdims=True)
    same = jnp.where((mine == named) & (u < v), 1, 0)
    slot = named * capacity + jnp.sum(same, axis=0, keepdims=True)
    place = jnp.where(
        lax.broadcasted_iota(jnp.int32, (slots, units), 0) == slot, 1.0, 0.0
    ).astype(BF)
    for j in range(8):
        even = rows[pl.ds(2 * j, units, stride=16), :]
        odd = rows[pl.ds(2 * j + 1, units, stride=16), :]
        unit = (even + odd).astype(BF)
        sent = jnp.dot(place, unit, preferred_element_type=F32)
        out[:, :, j * C : (j + 1) * C] = sent.reshape(strips, capacity, C).astype(BF)


VM = pl.BlockSpec(memory_space=pltpu.VMEM)
HB = pl.BlockSpec(memory_space=pltpu.HBM)


def field(*lead, dtype=BF):
    return jax.ShapeDtypeStruct((*lead, COLS, C), dtype)


def run(kernel, outs, args, units, scratch=None, in_specs=None):
    if scratch is None:
        scratch = [pltpu.VMEM((4, 12, COLS, C), BF)]
    single = not isinstance(outs, list)
    moved = sum(a.size * a.dtype.itemsize for a in args)
    return pl.pallas_call(
        kernel,
        out_shape=outs,
        in_specs=in_specs or [VM] * len(args),
        out_specs=VM if single else [VM] * len(outs),
        scratch_shapes=scratch,
        compiler_params=pltpu.CompilerParams(vmem_limit_bytes=40 << 20),
        cost_estimate=pl.CostEstimate(
            flops=units * COLS * 27 * C * C * 1, bytes_accessed=moved, transcendentals=0
        ),
        name=kernel.__name__,
    )(*args)


def in_hbm(x):
    return pltpu.with_memory_space_constraint(x, pltpu.HBM)


def on_device(pixel_cot, frame_group, advantage, block_in, conv1_weight, conv2_weight, owner_map):
    times, strips = lax.axis_size("tm"), lax.axis_size("space")

    inner_pairs = [(s, s ^ 1) for s in range(strips)]
    outer_pairs = [(s, (s + 1 if s % 2 else s - 1) % strips) for s in range(strips)]
    later = [((t + 1) % times, t) for t in range(times)]
    sooner = [(t, (t + 1) % times) for t in range(times)]

    def swap_in(x):
        return lax.ppermute(x, "space", inner_pairs)

    def swap_out(x):
        return lax.ppermute(x, "space", outer_pairs)

    def from_later(x):
        return lax.ppermute(x, "tm", later)

    def corner(x, steps, pairs):
        route = [(a * strips + s, b * strips + r) for a, b in steps for s, r in pairs]
        return lax.ppermute(x, ("tm", "space"), route)

    def from_sooner(x):
        return lax.ppermute(x, "tm", sooner)

    w1, w2 = conv1_weight, conv2_weight
    bi = block_in
    ext = pltpu.VMEM((4, 12, COLS, C), BF)

    ten, eight = field(2, 10, dtype=F32), field(2, 8, dtype=F32)
    edges = [field(2, 8), field(6), field(6)]

    v0, rin, rout, b1x, dpi, dpo = run(
        start_kernel,
        [
            field(4, 8), field(3, 4, 2), field(3, 4, 2), field(2, 8), field(2, 2), field(2, 2),
        ],
        tuple(in_hbm(x) for x in (pixel_cot, bi, frame_group, advantage)),
        1,
        scratch=[
            pltpu.VMEM((4, 8, COLS, C), BF),
            pltpu.SMEM(frame_group.shape, jnp.int32),
            pltpu.SMEM(advantage.shape, F32),
            pltpu.SemaphoreType.DMA((13,)),
        ],
        in_specs=[HB] * 4,
    )
    b1x = from_sooner(b1x)
    rout, rin = swap_out(rout), swap_in(rin)
    dpo, dpi = corner(dpo, sooner, outer_pairs), corner(dpi, sooner, inner_pairs)
    v0x = from_later(run(extend_kernel, field(2, 10), (v0, rin, rout), 1, scratch=[]))
    taps = jax.ShapeDtypeStruct((1, *w1.shape[1:]), BF)
    bi1, w2late, w1late = run(
        fetch_kernel,
        [field(4, 8), taps, taps],
        (v0, in_hbm(bi), in_hbm(w2), in_hbm(w1)),
        1,
        scratch=[pltpu.SemaphoreType.DMA((3,))],
        in_specs=[VM, HB, HB, HB],
    )
    ga, ga23, d1, pre = run(
        early_kernel,
        [ten, eight, eight, ten],
        (v0, bi1, rin, rout, w2late, w1late),
        54,
        scratch=[ext, ext],
    )
    v1x = run(
        pre01_kernel,
        field(2, 10),
        (b1x, dpi, dpo, ga, pre, w1),
        10,
        scratch=[pltpu.VMEM((2, 12, COLS, C), BF)],
    )
    v1xr = from_later(v1x)
    v1, ein, eout = run(pre23_kernel, edges, (ga23, v0x, d1, v1x, w2), 8)
    r1out, r1in = swap_out(eout), swap_in(ein)
    b0x = run(extend0_kernel, field(2, 12), (bi, rin, rout, v1), 1, scratch=[])
    b0x = from_sooner(b0x)
    base01, base23 = run(
        inner_up_kernel,
        [ten, eight],
        (v1x, v1, v0, rin, rout, w1),
        28,
        scratch=[ext, pltpu.VMEM((2, 12, COLS, C), BF)],
    )
    d0 = run(factor23_kernel, eight, (bi, rin, rout, base23, w1), 16)
    v2x = run(up01_kernel, field(2, 10), (base01, r1in, r1out, d0, w1), 8, scratch=[])
    v2xr = from_later(v2x)
    v2, ein, eout = run(up23_kernel, edges, (base23, r1in, r1out, v1xr, v2x, w1), 10)
    r2out, r2in = swap_out(eout), swap_in(ein)
    d0a = run(factor01_kernel, ten, (bi, rin, rout, b0x, v2, w1), 20)
    base01, base23 = run(inner_grad_kernel, [ten, eight], (v2x, v2, d0a, w2), 28)
    v3x = run(grad01_kernel, field(2, 10), (base01, r2in, r2out, d0a, w2), 8, scratch=[])
    v3xr = from_later(v3x)
    v3, ein, eout = run(
        grad23_kernel,
        [field(2, 8), field(2), field(2)],
        (base23, r2in, r2out, v2xr, d0, w2),
        10,
    )
    r3out, r3in = swap_out(eout), swap_in(ein)
    base = run(inner_last_kernel, field(4, 8, dtype=F32), (v3x, v3, v2x, v2, w1), 24)
    owner = owner_map.reshape(1, -1)
    units = owner.shape[1]
    capacity = max(2, 2 * units // strips)
    outgoing = run(
        last_kernel,
        jax.ShapeDtypeStruct((strips, capacity, 8 * C), BF),
        (base, r3in, r3out, v3xr, owner, w1),
        8,
        scratch=[ext, pltpu.VMEM((4 * 4 * COLS, C), F32)],
    )
    arrived = lax.all_to_all(outgoing, "space", split_axis=0, concat_axis=0, tiled=True)
    return arrived.reshape(1, 1, strips, capacity, 8 * C)


def solution(mesh):
    in_specs = (
        P("tm", "space", None, None),
        P("tm"),
        P(),
        P(None, "tm", "space", None, None),
        P(),
        P(),
        P("tm", "space", None, None),
    )
    out_specs = P("tm", "space", None, None, None)
    return jax.shard_map(
        on_device, mesh=mesh, in_specs=in_specs, out_specs=out_specs, check_vma=False
    )
```
